256 devices in a mesh: states: 256 (over x, y, z, core).
Axes of the slice: x: 4, y: 4, z: 8, core: 2. Of those that a mesh axis runs over, the one named last changes fastest.
Arguments:
- tiles: float32 [16, 256, 4, 128, 128], P(None, 'states'), may hold values from 0.001 to 1
- counts: int32 [256], P('states'), may hold values from 1 to 4
- col_index: int32 [256, 4], P('states'), may hold values from 0 to 255
- reward: float32 [16, 32768], P(None, 'states'), may hold values from -2.4 to 2.4
- policy: int32 [2, 32768], P(None, 'states'), may hold values from 0 to 15
- start_values: float32 [32768], P('states'), may hold values from -6 to 6
Outputs:
- final_values: float32 [32768], P('states')
- bounds: float32 [2, 2], replicated
The draws below stay inside these ranges and needn't reach their ends.
Inputs may be any that keep to these rules, and one draw needn't show every extreme that they name: Only the tile slots below counts of a row block enter W_a and row_total; slots at or above it hold arbitrary values that are ignored.
All inputs are finite; a program needn't handle non-finite values.
Results may differ from the reference program's by a relative error of at most 0.00014.
Values sent between devices are 32-bit elements; how exact they have to be, the bound alone decides.
No kernel may reach another device: no remote copies, remote signals or barrier semaphores. Data moves between devices by JAX's collectives and lax.ppermute only.
A program may use at most 64 MiB of HBM per device.

```python
import math
import jax
import jax.numpy as jnp
from jax import lax

A = 16
TILE = 128
KMAX = 4
SWEEPS = 2
EVALS = 2
NBLK = 256
S = 32768


def with_ends(array, own_key, least, largest):
    shape = array.shape
    index_at = [jax.random.randint(jax.random.fold_in(own_key, axis), (), 0, shape[axis]) for axis in range(len(shape))]
    array = array.at[tuple(index_at)].set(least)
    longest = shape.index(max(shape))
    index_at[longest] = (index_at[longest] + 1) % shape[longest]
    return array.at[tuple(index_at)].set(largest)


def block_levels(rng, extent, cuts, smallest, high):
    factor_of = 1.0
    for axis_at, shards_of in cuts:
        draws = jax.random.uniform(jax.random.fold_in(jax.random.fold_in(rng, 6), axis_at), (shards_of,), jnp.float32, smallest / len(cuts), high / len(cuts))
        factor_of = factor_of * jnp.repeat(jnp.exp(draws), extent[axis_at] // shards_of).reshape((-1,) + (1,) * (len(extent) - 1 - axis_at))
    return factor_of


def noise(stream_key, shape, deviation, limit, cuts=(), kind=jnp.bfloat16):
    values = jax.random.normal(stream_key, shape, jnp.float32) * deviation
    if len(cuts) > 0:
        values = block_levels(stream_key, shape, cuts, -0.22, 0.18) * values
    return jnp.clip(values, min=-limit, max=limit).astype(kind)


def setup_inputs(seed: int = 0) -> dict:
    streams_of = jax.random.split(jax.random.key(seed), 7)
    return {
        "tiles": jnp.clip(jnp.exp(math.log(1.0) - 6.9077552 * jax.random.uniform(streams_of[0], (A, NBLK, KMAX, TILE, TILE), jnp.float32) ** block_levels(streams_of[0], (A, NBLK, KMAX, TILE, TILE), ((1, 256),), -0.2, 0.2)), 0.001, 1.0),
        "counts": with_ends(jax.random.randint(streams_of[1], (NBLK,), 1, KMAX + 1), jax.random.fold_in(streams_of[1], 1), 1, KMAX).astype(jnp.int32),
        "col_index": with_ends(jax.random.randint(streams_of[2], (NBLK, KMAX), 0, NBLK), jax.random.fold_in(streams_of[2], 1), 0, NBLK - 1).astype(jnp.int32),
        "reward": noise(streams_of[3], (A, S), 0.3, 2.4, ((1, 256),), jnp.float32),
        "policy": with_ends(jax.random.randint(streams_of[4], (SWEEPS, S), 0, A), jax.random.fold_in(streams_of[4], 1), 0, A - 1).astype(jnp.int32),
        "start_values": noise(streams_of[5], (S,), 1.0, 6.0, ((0, 256),), jnp.float32),
    }


discount = 0.9
precise = lax.Precision.HIGHEST


def reference(tiles, counts, col_index, reward, policy, start_values):
    live_mask = (jnp.arange(KMAX)[None, :] < counts[:, None]).astype(jnp.float32)
    row_total = jnp.einsum("abkrc,bk->abr", tiles, live_mask, precision=precise)

    def fetch(vector):
        blocks = vector.reshape(NBLK, TILE)[col_index]
        return blocks * live_mask[:, :, None]

    values = start_values
    bound_rows = []
    for sweep_index in range(SWEEPS):
        weighted = jnp.einsum("abkrc,bkc->abr", tiles, fetch(values), precision=precise)
        action_values = reward + discount * (weighted / row_total).reshape(A, S)
        backup = jnp.max(action_values, axis=0)
        change = backup - values
        top_bound = jnp.max(change)
        bottom = jnp.min(change)
        bound_rows.append(jnp.stack([bottom, top_bound]))
        offset = discount / (1.0 - discount) * 0.5 * (bottom + top_bound)
        onehot = (policy[sweep_index][None, :] == jnp.arange(A)[:, None]).astype(jnp.float32)
        onehot_blocks = onehot.reshape(A, NBLK, TILE)
        picked = jnp.einsum("abr,abkrc->bkrc", onehot_blocks, tiles, precision=precise)
        picked_total = jnp.sum(onehot_blocks * row_total, axis=0)
        picked_reward = jnp.sum(onehot * reward, axis=0)
        current = backup + offset
        for eval_turn in range(EVALS):
            weighted = jnp.einsum("bkrc,bkc->br", picked, fetch(current), precision=precise)
            current = picked_reward + discount * (weighted / picked_total).reshape(S)
        values = current
    return values, jnp.stack(bound_rows)
```

```python
import functools

import jax
import jax.numpy as jnp
from jax import lax
from jax.experimental import pallas as pl
from jax.experimental.pallas import tpu as pltpu
from jax.sharding import Mesh
from jax.sharding import PartitionSpec as P

SWEEPS = 2
EVALS = 2
AXES = ("x", "y", "z", "c")
discount = 0.9
shift = discount / (1.0 - discount) * 0.5
MIB = 1 << 20


def piece_sums(rows, values):
    high = values.astype(jnp.bfloat16)
    rest = values - high.astype(jnp.float32)
    middle = rest.astype(jnp.bfloat16)
    low = (rest - middle.astype(jnp.float32)).astype(jnp.bfloat16)
    dims = (((1,), (1,)), ((), ()))
    out = lax.dot_general(rows, high, dims, preferred_element_type=jnp.float32)
    out += lax.dot_general(rows, middle, dims, preferred_element_type=jnp.float32)
    return out + lax.dot_general(rows, low, dims, preferred_element_type=jnp.float32)


def row_of(index):
    at = lax.broadcasted_iota(jnp.int32, (16, 128), 0)
    return jnp.where(at == index, 1.0, 0.0).astype(jnp.bfloat16)


def prepare(counts, policy, reward, tiles, scale, picked, picked_scale, picked_reward, sums, columns):
    actions, slots, width, _ = tiles.shape
    for j in range(SWEEPS):
        wide = jnp.broadcast_to(policy[pl.ds(j, 1), :].astype(jnp.float32), (width, width))
        columns[j] = wide.T
    live = [counts[0] > k for k in range(slots)]

    def group(g, _):
        rows = pl.ds(pl.multiple_of(g * 8, 8), 8)
        chosen = [columns[j, rows, :] for j in range(SWEEPS)]
        held = [[jnp.zeros((8, width), jnp.float32) for _ in range(slots)] for _ in range(SWEEPS)]
        for a in range(actions):
            total = jnp.zeros((8, width), jnp.float32)
            for k in range(slots):
                tile = jnp.where(live[k], tiles[a, k, rows, :], 0.0)
                total += tile
                for j in range(SWEEPS):
                    held[j][k] = jnp.where(chosen[j] == float(a), tile, held[j][k])
            sums[a, rows, :] = total
        for j in range(SWEEPS):
            for k in range(slots):
                picked[j, k, rows, :] = held[j][k]
        return 0

    lax.fori_loop(0, width // 8, group, 0)
    totals = jnp.zeros((actions, width), jnp.float32)
    for a in range(actions):
        totals += piece_sums(row_of(a), sums[a])
    inverse = discount / totals
    scale[...] = inverse
    at = lax.broadcasted_iota(jnp.int32, (actions, width), 0)
    for j in range(SWEEPS):
        here = at == policy[pl.ds(j, 1), :]
        picked_scale[pl.ds(j, 1), :] = jnp.sum(jnp.where(here, inverse, 0.0), axis=0, keepdims=True)
        picked_reward[pl.ds(j, 1), :] = jnp.sum(jnp.where(here, reward[...], 0.0), axis=0, keepdims=True)


def fetched(counts, col_index, gathered, slots):
    out = []
    for k in range(slots):
        row = gathered[pl.ds(col_index[0, k], 1), :]
        out.append(jnp.where(counts[0] > k, row, 0.0))
    return out


def back_up(counts, col_index, gathered, tiles, reward, scale, out, sums):
    actions, slots, width, _ = tiles.shape
    blocks = [jnp.broadcast_to(b, (8, width)) for b in fetched(counts, col_index, gathered, slots)]

    def group(g, _):
        rows = pl.ds(pl.multiple_of(g * 8, 8), 8)
        for a in range(actions):
            total = tiles[a, 0, rows, :] * blocks[0]
            for k in range(1, slots):
                total += tiles[a, k, rows, :] * blocks[k]
            sums[a, rows, :] = total
        return 0

    lax.fori_loop(0, width // 8, group, 0)
    weighted = jnp.zeros((actions, width), jnp.float32)
    for a in range(actions):
        weighted += piece_sums(row_of(a), sums[a])
    backup = jnp.max(reward[...] + scale[...] * weighted, axis=0, keepdims=True)
    out[...] = jnp.broadcast_to(backup, out.shape)


def product(counts, col_index, gathered, picked, scale, reward):
    slots, width, _ = picked.shape
    blocks = fetched(counts, col_index, gathered, slots)
    total = picked[0] * blocks[0]
    for k in range(1, slots):
        total += picked[k] * blocks[k]
    weighted = piece_sums(jnp.ones((16, width), jnp.bfloat16), total)[0:1]
    return reward + scale * weighted


def first_evaluation(j, counts, col_index, gathered, before, held, picked, scale, reward, out, bounds):
    change = gathered[...] - before[...]
    top = jnp.max(change)
    bottom = jnp.min(change)
    offset = shift * (bottom + top)
    got = product(counts, col_index, gathered, picked.at[j], scale[pl.ds(j, 1), :], reward[pl.ds(j, 1), :])
    out[...] = jnp.broadcast_to(got + discount * offset, out.shape)
    sweep = lax.broadcasted_iota(jnp.int32, bounds.shape, 0)
    side = lax.broadcasted_iota(jnp.int32, bounds.shape, 1)
    bounds[...] = jnp.where(sweep < j, held[...], jnp.where(side == 0, bottom, top))


def last_evaluation(j, counts, col_index, gathered, picked, scale, reward, bounds, out, bound_rows):
    got = product(counts, col_index, gathered, picked.at[j], scale[pl.ds(j, 1), :], reward[pl.ds(j, 1), :])
    out[...] = jnp.broadcast_to(got, out.shape)
    bound_rows[...] = bounds[...]


def next_evaluation(j, counts, col_index, gathered, picked, scale, reward, out):
    got = product(counts, col_index, gathered, picked.at[j], scale[pl.ds(j, 1), :], reward[pl.ds(j, 1), :])
    out[...] = jnp.broadcast_to(got, out.shape)


SCALARS = pl.BlockSpec(memory_space=pltpu.SMEM)
VECTORS = pl.BlockSpec(memory_space=pltpu.VMEM)


def shaped(*shape):
    return jax.ShapeDtypeStruct(shape, jnp.float32)


def exchange(rows):
    return lax.all_to_all(rows, AXES, 0, 0, tiled=True)


def local(tiles, counts, col_index, reward, policy, start_values):
    actions, _, slots, width, _ = tiles.shape
    devices = lax.axis_size(AXES)
    tiles = tiles.reshape(actions, slots, width, width)
    gathered = exchange(jnp.broadcast_to(start_values[None], (devices, width)))
    params = pltpu.CompilerParams(vmem_limit_bytes=12 * MIB)
    scale, picked, picked_scale, picked_reward = pl.pallas_call(
        prepare,
        out_shape=(shaped(actions, width), shaped(SWEEPS, slots, width, width), shaped(SWEEPS, width), shaped(SWEEPS, width)),
        in_specs=[SCALARS, VECTORS, VECTORS, VECTORS],
        out_specs=(VECTORS,) * 4,
        scratch_shapes=[
            pltpu.VMEM((actions, width, width), jnp.float32),
            pltpu.VMEM((SWEEPS, width, width), jnp.float32),
        ],
        compiler_params=params,
        cost_estimate=pl.CostEstimate(flops=4_000_000, bytes_accessed=6_000_000, transcendentals=0),
        name="prepare",
    )(counts, policy, reward, tiles)

    def called(body, out_shape, scratch, name):
        return pl.pallas_call(
            body,
            out_shape=out_shape,
            in_specs=[SCALARS, SCALARS] + [VECTORS] * (len(given) - 2),
            out_specs=jax.tree.map(lambda _: VECTORS, out_shape),
            scratch_shapes=scratch,
            compiler_params=params,
            name=name,
        )(*given)

    bounds = jnp.zeros((SWEEPS, 2), jnp.float32)
    all_rows = shaped(devices, width)
    for j in range(SWEEPS):
        given = (counts, col_index, gathered, tiles, reward, scale)
        backup = called(back_up, all_rows, [pltpu.VMEM((actions, width, width), jnp.float32)], f"back_up_{j}")
        before, gathered = gathered, exchange(backup)
        given = (counts, col_index, gathered, before, bounds, picked, picked_scale, picked_reward)
        body = functools.partial(first_evaluation, j)
        current, bounds = called(body, (all_rows, shaped(SWEEPS, 2)), [], f"first_evaluation_{j}")
        gathered = exchange(current)
        given = (counts, col_index, gathered, picked, picked_scale, picked_reward)
        if j < SWEEPS - 1:
            gathered = exchange(called(functools.partial(next_evaluation, j), all_rows, [], f"next_evaluation_{j}"))
    given += (bounds,)
    body = functools.partial(last_evaluation, SWEEPS - 1)
    current, bounds = called(body, (shaped(1, width), shaped(SWEEPS, 2)), [], "last_evaluation")
    return current.reshape(width), bounds


def solution(mesh):
    split = Mesh(mesh.devices.reshape(4, 4, 8, 2), AXES)
    placed = (
        P(None, AXES, None, None, None),
        P(AXES),
        P(AXES, None),
        P(None, AXES),
        P(None, AXES),
        P(AXES),
    )
    return jax.shard_map(local, mesh=split, in_specs=placed, out_specs=(P(AXES), P()), check_vma=False)
```

```python
import functools

import jax
import jax.numpy as jnp
from jax import lax
from jax.experimental import pallas as pl
from jax.experimental.pallas import tpu as pltpu
from jax.sharding import Mesh
from jax.sharding import PartitionSpec as P

SWEEPS = 2
EVALS = 2
AXES = ("x", "y", "z", "c")
discount = 0.9
shift = discount / (1.0 - discount) * 0.5
MIB = 1 << 20


def piece_sums(rows, values):
    high = values.astype(jnp.bfloat16)
    rest = values - high.astype(jnp.float32)
    middle = rest.astype(jnp.bfloat16)
    low = (rest - middle.astype(jnp.float32)).astype(jnp.bfloat16)
    dims = (((1,), (1,)), ((), ()))
    out = lax.dot_general(rows, high, dims, preferred_element_type=jnp.float32)
    out += lax.dot_general(rows, middle, dims, preferred_element_type=jnp.float32)
    return out + lax.dot_general(rows, low, dims, preferred_element_type=jnp.float32)


def row_of(index):
    at = lax.broadcasted_iota(jnp.int32, (16, 128), 0)
    return jnp.where(at == index, 1.0, 0.0).astype(jnp.bfloat16)


def spread(counts, col_index, start, out, table):
    for k in range(table.shape[1]):
        table[0, k] = jnp.where(counts[0] > k, col_index[0, k], -1)
    out[...] = jnp.broadcast_to(start[...], out.shape)


def fetched(table, gathered):
    out = []
    for k in range(table.shape[1]):
        at = table[0, k]
        row = gathered[pl.ds(jnp.maximum(at, 0), 1), :]
        out.append(jnp.where(at >= 0, row, 0.0))
    return out


def first_back_up(
    table, gathered, tiles, reward, policy, out, scale, picked, picked_scale, picked_reward, sums, weights, columns
):
    actions, slots, width, _ = tiles.shape
    for j in range(SWEEPS):
        columns[j] = jnp.broadcast_to(policy[pl.ds(j, 1), :].astype(jnp.float32), (width, width)).T
    live = [table[0, k] >= 0 for k in range(slots)]
    blocks = [jnp.broadcast_to(b, (8, width)) for b in fetched(table, gathered)]

    def group(g, _):
        rows = pl.ds(pl.multiple_of(g * 8, 8), 8)
        chosen = [columns[j, rows, :] for j in range(SWEEPS)]
        held = [[jnp.zeros((8, width), jnp.float32) for _ in range(slots)] for _ in range(SWEEPS)]
        for a in range(actions):
            total = jnp.zeros((8, width), jnp.float32)
            weighted = jnp.zeros((8, width), jnp.float32)
            for k in range(slots):
                tile = jnp.where(live[k], tiles[a, k, rows, :], 0.0)
                total += tile
                weighted += tile * blocks[k]
                for j in range(SWEEPS):
                    held[j][k] = jnp.where(chosen[j] == float(a), tile, held[j][k])
            sums[a, rows, :] = total
            weights[a, rows, :] = weighted
        for j in range(SWEEPS):
            for k in range(slots):
                picked[j, k, rows, :] = held[j][k]
        return 0

    lax.fori_loop(0, width // 8, group, 0)
    totals = jnp.zeros((actions, width), jnp.float32)
    weighted = jnp.zeros((actions, width), jnp.float32)
    for a in range(actions):
        totals += piece_sums(row_of(a), sums[a])
        weighted += piece_sums(row_of(a), weights[a])
    inverse = discount / totals
    scale[...] = inverse
    backup = jnp.max(reward[...] + inverse * weighted, axis=0, keepdims=True)
    out[...] = jnp.broadcast_to(backup, out.shape)
    at = lax.broadcasted_iota(jnp.int32, (actions, width), 0)
    for j in range(SWEEPS):
        here = at == policy[pl.ds(j, 1), :]
        picked_scale[pl.ds(j, 1), :] = jnp.sum(jnp.where(here, inverse, 0.0), axis=0, keepdims=True)
        picked_reward[pl.ds(j, 1), :] = jnp.sum(jnp.where(here, reward[...], 0.0), axis=0, keepdims=True)


def back_up(table, gathered, tiles, reward, scale, out, sums):
    actions, slots, width, _ = tiles.shape
    blocks = [jnp.broadcast_to(b, (8, width)) for b in fetched(table, gathered)]

    def group(g, _):
        rows = pl.ds(pl.multiple_of(g * 8, 8), 8)
        for a in range(actions):
            total = tiles[a, 0, rows, :] * blocks[0]
            for k in range(1, slots):
                total += tiles[a, k, rows, :] * blocks[k]
            sums[a, rows, :] = total
        return 0

    lax.fori_loop(0, width // 8, group, 0)
    weighted = jnp.zeros((actions, width), jnp.float32)
    for a in range(actions):
        weighted += piece_sums(row_of(a), sums[a])
    backup = jnp.max(reward[...] + scale[...] * weighted, axis=0, keepdims=True)
    out[...] = jnp.broadcast_to(backup, out.shape)


def product(table, gathered, picked, scale, reward):
    slots, width, _ = picked.shape
    blocks = fetched(table, gathered)
    total = picked[0] * blocks[0]
    for k in range(1, slots):
        total += picked[k] * blocks[k]
    weighted = piece_sums(jnp.ones((16, width), jnp.bfloat16), total)[0:1]
    return reward + scale * weighted


def first_evaluation(j, table, gathered, before, held, picked, scale, reward, out, bounds):
    change = gathered[...] - before[...]
    top = jnp.max(change)
    bottom = jnp.min(change)
    offset = shift * (bottom + top)
    got = product(table, gathered, picked.at[j], scale[pl.ds(j, 1), :], reward[pl.ds(j, 1), :])
    out[...] = jnp.broadcast_to(got + discount * offset, out.shape)
    sweep = lax.broadcasted_iota(jnp.int32, bounds.shape, 0)
    side = lax.broadcasted_iota(jnp.int32, bounds.shape, 1)
    bounds[...] = jnp.where(sweep < j, held[...], jnp.where(side == 0, bottom, top))


def last_evaluation(j, table, gathered, picked, scale, reward, bounds, out, bound_rows):
    got = product(table, gathered, picked.at[j], scale[pl.ds(j, 1), :], reward[pl.ds(j, 1), :])
    out[...] = jnp.broadcast_to(got, out.shape)
    bound_rows[...] = bounds[...]


def next_evaluation(j, table, gathered, picked, scale, reward, out):
    got = product(table, gathered, picked.at[j], scale[pl.ds(j, 1), :], reward[pl.ds(j, 1), :])
    out[...] = jnp.broadcast_to(got, out.shape)


SCALARS = pl.BlockSpec(memory_space=pltpu.SMEM)
VECTORS = pl.BlockSpec(memory_space=pltpu.VMEM)


def shaped(*shape):
    return jax.ShapeDtypeStruct(shape, jnp.float32)


def exchange(rows):
    return lax.all_to_all(rows, AXES, 0, 0, tiled=True)


def local(tiles, counts, col_index, reward, policy, start_values):
    actions, _, slots, width, _ = tiles.shape
    devices = lax.axis_size(AXES)
    tiles = tiles.reshape(actions, slots, width, width)
    rows, table = pl.pallas_call(
        spread,
        out_shape=(shaped(devices, width), jax.ShapeDtypeStruct(col_index.shape, jnp.int32)),
        in_specs=[SCALARS, SCALARS, VECTORS],
        out_specs=(VECTORS, SCALARS),
        compiler_params=pltpu.CompilerParams(vmem_limit_bytes=2 * MIB),
        name="spread",
    )(counts, col_index, start_values.reshape(1, width))
    gathered = exchange(rows)
    params = pltpu.CompilerParams(vmem_limit_bytes=12 * MIB)
    def called(body, out_shape, scratch, name):
        return pl.pallas_call(
            body,
            out_shape=out_shape,
            in_specs=[SCALARS] + [VECTORS] * (len(given) - 1),
            out_specs=jax.tree.map(lambda _: VECTORS, out_shape),
            scratch_shapes=scratch,
            compiler_params=params,
            name=name,
        )(*given)

    bounds = jnp.zeros((SWEEPS, 2), jnp.float32)
    all_rows = shaped(devices, width)
    square = pltpu.VMEM((actions, width, width), jnp.float32)
    for j in range(SWEEPS):
        if j == 0:
            given = (table, gathered, tiles, reward, policy)
            made = (
                all_rows,
                shaped(actions, width),
                shaped(SWEEPS, slots, width, width),
                shaped(SWEEPS, width),
                shaped(SWEEPS, width),
            )
            scratch = [square, square, pltpu.VMEM((SWEEPS, width, width), jnp.float32)]
            backup, scale, picked, picked_scale, picked_reward = called(first_back_up, made, scratch, "first_back_up")
        else:
            given = (table, gathered, tiles, reward, scale)
            backup = called(back_up, all_rows, [square], f"back_up_{j}")
        before, gathered = gathered, exchange(backup)
        given = (table, gathered, before, bounds, picked, picked_scale, picked_reward)
        body = functools.partial(first_evaluation, j)
        current, bounds = called(body, (all_rows, shaped(SWEEPS, 2)), [], f"first_evaluation_{j}")
        gathered = exchange(current)
        given = (table, gathered, picked, picked_scale, picked_reward)
        if j < SWEEPS - 1:
            gathered = exchange(called(functools.partial(next_evaluation, j), all_rows, [], f"next_evaluation_{j}"))
    given += (bounds,)
    body = functools.partial(last_evaluation, SWEEPS - 1)
    current, bounds = called(body, (shaped(1, width), shaped(SWEEPS, 2)), [], "last_evaluation")
    return current.reshape(width), bounds


def solution(mesh):
    split = Mesh(mesh.devices.reshape(4, 4, 8, 2), AXES)
    placed = (
        P(None, AXES, None, None, None),
        P(AXES),
        P(AXES, None),
        P(None, AXES),
        P(None, AXES),
        P(AXES),
    )
    return jax.shard_map(local, mesh=split, in_specs=placed, out_specs=(P(AXES), P()), check_vma=False)
```

```python
import functools

import jax
import jax.numpy as jnp
from jax import lax
from jax.experimental import pallas as pl
from jax.experimental.pallas import tpu as pltpu
from jax.sharding import Mesh
from jax.sharding import PartitionSpec as P

SWEEPS = 2
AXES = ("x", "y", "z", "c")
ORDER = ("x", "y", "c", "z")
PLANE = ("x", "y", "c")
LINE = "z"
discount = 0.9
shift = discount / (1.0 - discount) * 0.5
MIB = 1 << 20
AUX = 8


def pieces(values):
    high = values.astype(jnp.bfloat16)
    rest = values - high.astype(jnp.float32)
    middle = rest.astype(jnp.bfloat16)
    low = (rest - middle.astype(jnp.float32)).astype(jnp.bfloat16)
    return high, middle, low


def contract(left, right, dims):
    out = None
    for piece in pieces(right):
        term = lax.dot_general(left, piece, (dims, ((), ())), preferred_element_type=jnp.float32)
        out = term if out is None else out + term
    return out


def lane_sums(count, row_values):
    at = lax.broadcasted_iota(jnp.int32, (16, 128), 0)
    out = jnp.zeros((16, 128), jnp.float32)
    for i in range(count):
        row = jnp.where(at == i, 1.0, 0.0).astype(jnp.bfloat16)
        out += contract(row, row_values(i), ((1,), (1,)))
    return out


def stacked(rows, height):
    at = lax.broadcasted_iota(jnp.int32, (height, rows[0].shape[-1]), 0)
    out = jnp.zeros(at.shape, jnp.float32)
    for i, row in enumerate(rows):
        out = jnp.where(at == i, row, out)
    return out


def prepare(counts, col_index, start, policy, reward, tiles, rows_out, table, scale, load_0, load_1, held_tiles, sums, columns, sems):
    actions, slots, width, _ = tiles.shape
    loads = (load_0, load_1)

    def copy(g):
        rows = pl.ds(pl.multiple_of(g * 8, 8), 8)
        return pltpu.make_async_copy(tiles.at[:, :, rows, :], held_tiles.at[:, :, rows, :], sems.at[g])

    for g in range(width // 8):
        copy(g).start()
    columns_of = []
    for k in range(slots):
        block = col_index[0, k]
        place = (block // 16) * 16 + (block % 2) * 8 + (block % 16) // 2
        place = jnp.where(counts[0] > k, place, -1)
        table[0, k] = place
        columns_of.append(jnp.full((1, width), place.astype(jnp.float32)))
    live = [counts[0] > k for k in range(slots)]
    rows_out[...] = jnp.broadcast_to(start[...], rows_out.shape)
    for j in range(SWEEPS):
        columns[j] = jnp.broadcast_to(policy[pl.ds(j, 1), :].astype(jnp.float32), (width, width)).T

    def group(g, _):
        rows = pl.ds(pl.multiple_of(g * 8, 8), 8)
        copy(g).wait()
        chosen = [columns[j, rows, :] for j in range(SWEEPS)]
        held = [[jnp.zeros((8, width), jnp.float32) for _ in range(slots)] for _ in range(SWEEPS)]
        for a in range(actions):
            total = jnp.zeros((8, width), jnp.float32)
            for k in range(slots):
                tile = jnp.where(live[k], held_tiles[a, k, rows, :], 0.0)
                total += tile
                for j in range(SWEEPS):
                    held[j][k] = jnp.where(chosen[j] == float(a), tile, held[j][k])
            sums[a, rows, :] = total
        for j in range(SWEEPS):
            for k in range(slots):
                loads[j][pl.ds(pl.multiple_of(k * width + g * 8, 8), 8), :] = held[j][k]
        return 0

    lax.fori_loop(0, width // 8, group, 0)
    inverse = discount / lane_sums(actions, lambda a: sums[a])
    scale[...] = inverse
    at = lax.broadcasted_iota(jnp.int32, (actions, width), 0)
    for j in range(SWEEPS):
        here = at == policy[pl.ds(j, 1), :]
        picked_scale = jnp.sum(jnp.where(here, inverse, 0.0), axis=0, keepdims=True)
        picked_reward = jnp.sum(jnp.where(here, reward[...], 0.0), axis=0, keepdims=True)
        loads[j][pl.ds(slots * width, AUX), :] = stacked([picked_scale, picked_reward] + columns_of, AUX)


def fetched(table, gathered):
    out = []
    for k in range(table.shape[1]):
        at = table[0, k]
        row = gathered[pl.ds(jnp.maximum(at, 0), 1), :]
        out.append(jnp.where(at >= 0, row, 0.0))
    return out


def back_up(table, gathered, tiles, reward, scale, out, sums):
    actions, slots, width, _ = tiles.shape
    blocks = [jnp.broadcast_to(b, (8, width)) for b in fetched(table, gathered)]

    def group(g, _):
        rows = pl.ds(pl.multiple_of(g * 8, 8), 8)
        for a in range(actions):
            total = tiles[a, 0, rows, :] * blocks[0]
            for k in range(1, slots):
                total += tiles[a, k, rows, :] * blocks[k]
            sums[a, rows, :] = total
        return 0

    lax.fori_loop(0, width // 8, group, 0)
    weighted = lane_sums(actions, lambda a: sums[a])
    backup = jnp.max(reward[...] + scale[...] * weighted, axis=0, keepdims=True)
    out[...] = jnp.broadcast_to(backup, out.shape)


def line_product(gathered, loads):
    states, width = gathered.shape
    high = width * 4 + AUX
    blocks = loads.shape[0] // high
    aux = [loads[pl.ds(b * high + 4 * width, AUX), :] for b in range(blocks)]
    named = jnp.concatenate(aux, axis=0)
    lane = lax.broadcasted_iota(jnp.int32, named.shape, 1).astype(jnp.float32)
    fetched_rows = None
    for h in range(states // width):
        chosen = jnp.where(named == lane + float(h * width), 1.0, 0.0).astype(jnp.bfloat16)
        term = contract(chosen, gathered[pl.ds(h * width, width), :], ((1,), (0,)))
        fetched_rows = term if fetched_rows is None else fetched_rows + term

    def weighted_rows(b):
        total = None
        for k in range(4):
            at = b * AUX + 2 + k
            term = loads[pl.ds(b * high + k * width, width), :] * fetched_rows[at : at + 1]
            total = term if total is None else total + term
        return total

    weighted = lane_sums(blocks, weighted_rows)[:blocks]
    scale = stacked([a[0:1] for a in aux], blocks)
    reward = stacked([a[1:2] for a in aux], blocks)
    return reward + scale * weighted


def spread_out(out, got):
    for i in range(out.shape[0] // got.shape[0]):
        out[pl.ds(i * got.shape[0], got.shape[0]), :] = got


def first_evaluation(j, gathered, before, held, loads, out, bounds):
    change = gathered[...] - before[...]
    top = jnp.max(change)
    bottom = jnp.min(change)
    offset = shift * (bottom + top)
    spread_out(out, line_product(gathered, loads) + discount * offset)
    sweep = lax.broadcasted_iota(jnp.int32, bounds.shape, 0)
    side = lax.broadcasted_iota(jnp.int32, bounds.shape, 1)
    bounds[...] = jnp.where(sweep < j, held[...], jnp.where(side == 0, bottom, top))


def next_evaluation(gathered, loads, out):
    spread_out(out, line_product(gathered, loads))


def last_evaluation(table, gathered, load, held, out, bounds):
    slots, width = table.shape[1], gathered.shape[1]
    blocks = fetched(table, gathered)
    total = load[pl.ds(0, width), :] * blocks[0]
    for k in range(1, slots):
        total += load[pl.ds(k * width, width), :] * blocks[k]
    weighted = lane_sums(1, lambda _: total)[0:1]
    aux = load[pl.ds(slots * width, AUX), :]
    out[...] = aux[1:2] + aux[0:1] * weighted
    bounds[...] = held[...]


SCALARS = pl.BlockSpec(memory_space=pltpu.SMEM)
VECTORS = pl.BlockSpec(memory_space=pltpu.VMEM)
LEFT = pl.BlockSpec(memory_space=pltpu.HBM)


def shaped(*shape):
    return jax.ShapeDtypeStruct(shape, jnp.float32)


def called(body, given, out_shape, name, scratch=(), scalars=0, limit=8):
    return pl.pallas_call(
        body,
        out_shape=out_shape,
        in_specs=[SCALARS] * scalars + [VECTORS] * (len(given) - scalars),
        out_specs=jax.tree.map(lambda _: VECTORS, out_shape),
        scratch_shapes=list(scratch),
        compiler_params=pltpu.CompilerParams(vmem_limit_bytes=limit * MIB),
        name=name,
    )(*given)


def over_all(rows):
    return lax.all_to_all(rows, ORDER, 0, 0, tiled=True)


def over_plane(rows):
    return lax.all_to_all(rows, PLANE, 0, 0, tiled=True)


def over_line(load):
    return lax.all_gather(load, LINE, axis=0, tiled=True)


def local(tiles, counts, col_index, reward, policy, start_values):
    actions, _, slots, width, _ = tiles.shape
    devices = lax.axis_size(AXES)
    tiles = tiles.reshape(actions, slots, width, width)
    all_rows = shaped(devices, width)
    load = shaped(slots * width + AUX, width)
    square = pltpu.VMEM((actions, width, width), jnp.float32)
    rows, table, scale, load_0, load_1, held_tiles = pl.pallas_call(
        prepare,
        out_shape=(
            all_rows,
            jax.ShapeDtypeStruct(col_index.shape, jnp.int32),
            shaped(actions, width),
            load,
            load,
            shaped(*tiles.shape),
        ),
        in_specs=[SCALARS, SCALARS, VECTORS, VECTORS, VECTORS, LEFT],
        out_specs=(VECTORS, SCALARS, VECTORS, VECTORS, VECTORS, VECTORS),
        scratch_shapes=[square, pltpu.VMEM((SWEEPS, width, width), jnp.float32), pltpu.SemaphoreType.DMA((width // 8,))],
        compiler_params=pltpu.CompilerParams(vmem_limit_bytes=12 * MIB),
        name="prepare",
    )(counts, col_index, start_values.reshape(1, width), policy, reward, tiles)

    loads = over_line(load_0)
    gathered = over_all(rows)
    bounds = jnp.zeros((SWEEPS, 2), jnp.float32)
    for j in range(SWEEPS):
        backup = called(back_up, (table, gathered, held_tiles, reward, scale), all_rows, f"back_up_{j}", [square], 1)
        before, gathered = gathered, over_all(backup)
        if j == 0:
            load_1, gathered = lax.optimization_barrier((load_1, gathered))
            later_loads = over_line(load_1)
        body = functools.partial(first_evaluation, j)
        given = (gathered, before, bounds, loads)
        current, bounds = called(body, given, (all_rows, shaped(SWEEPS, 2)), f"first_evaluation_{j}")
        gathered = over_plane(current)
        if j < SWEEPS - 1:
            current = called(next_evaluation, (gathered, loads), all_rows, f"next_evaluation_{j}")
            gathered = over_plane(current)
            loads = later_loads
    given = (table, gathered, load_1, bounds)
    current, bounds = called(last_evaluation, given, (shaped(1, width), shaped(SWEEPS, 2)), "last_evaluation", (), 1)
    return current.reshape(width), bounds


def solution(mesh):
    split = Mesh(mesh.devices.reshape(4, 4, 8, 2), AXES)
    placed = (
        P(None, AXES, None, None, None),
        P(AXES),
        P(AXES, None),
        P(None, AXES),
        P(None, AXES),
        P(AXES),
    )
    return jax.shard_map(local, mesh=split, in_specs=placed, out_specs=(P(AXES), P()), check_vma=False)
```

```python
import functools

import jax
import jax.numpy as jnp
from jax import lax
from jax.experimental import pallas as pl
from jax.experimental.pallas import tpu as pltpu
from jax.sharding import Mesh
from jax.sharding import PartitionSpec as P

SWEEPS = 2
AXES = ("x", "y", "z", "c")
ORDER = ("x", "y", "c", "z")
PLANE = ("x", "y", "c")
LINE = "z"
discount = 0.9
shift = discount / (1.0 - discount) * 0.5
MIB = 1 << 20
AUX = 8
CHUNK = 16
KEEP = True


def pieces(values, count):
    out = []
    for left in reversed(range(count)):
        piece = values.astype(jnp.bfloat16)
        out.append(piece)
        if left:
            values = values - piece.astype(jnp.float32)
    return out


def contract(left, right, dims, count):
    out = None
    for piece in pieces(right, count):
        term = lax.dot_general(left, piece, (dims, ((), ())), preferred_element_type=jnp.float32)
        out = term if out is None else out + term
    return out


def lane_sums(count, row_values):
    at = lax.broadcasted_iota(jnp.int32, (16, 128), 0)
    out = jnp.zeros((16, 128), jnp.float32)
    for i in range(count):
        row = jnp.where(at == i, 1.0, 0.0).astype(jnp.bfloat16)
        out += contract(row, row_values(i), ((1,), (1,)), 2)
    return out


def stacked(rows, height):
    at = lax.broadcasted_iota(jnp.int32, (height, rows[0].shape[-1]), 0)
    out = jnp.zeros(at.shape, jnp.float32)
    for i, row in enumerate(rows):
        out = jnp.where(at == i, row, out)
    return out


def chunk(g, tiles, held_tiles, sems):
    rows = pl.ds(g * CHUNK, CHUNK)
    return pltpu.make_async_copy(tiles.at[:, :, rows, :], held_tiles.at[:, :, rows, :], sems.at[g])


def prepare(
    counts, columns_in, start_in, policy_in, reward_in, tiles,
    rows_out, table, scale, load_0, load_1,
    col_index, start, policy, reward, held_tiles, sums, columns, sems, small_sems,
):
    actions, slots, width, _ = tiles.shape
    loads = (load_0, load_1)
    given = ((columns_in, col_index), (start_in, start), (policy_in, policy), (reward_in, reward))
    small = [pltpu.make_async_copy(source, target, small_sems.at[i]) for i, (source, target) in enumerate(given)]
    for copy in small:
        copy.start()
    for g in range(width // CHUNK):
        chunk(g, tiles, held_tiles, sems).start()
    for copy in small:
        copy.wait()
    rows_out[...] = jnp.broadcast_to(start[...], rows_out.shape)
    columns_of = []
    for k in range(slots):
        block = col_index[0, k]
        place = (block // 16) * 16 + (block % 2) * 8 + (block % 16) // 2
        place = jnp.where(counts[0] > k, place, -1)
        table[0, k] = place
        columns_of.append(jnp.full((1, width), place.astype(jnp.float32)))
    live = [counts[0] > k for k in range(slots)]
    for j in range(SWEEPS):
        columns[j] = jnp.broadcast_to(policy[pl.ds(j, 1), :].astype(jnp.float32), (width, width)).T
    for g in range(width // CHUNK):
        chunk(g, tiles, held_tiles, sems).wait()
        for r in range(g * CHUNK, (g + 1) * CHUNK, 8):
            rows = pl.ds(r, 8)
            chosen = [columns[j, rows, :] for j in range(SWEEPS)]
            held = [[jnp.zeros((8, width), jnp.float32) for _ in range(slots)] for _ in range(SWEEPS)]
            for a in range(actions):
                total = None
                for k in range(slots):
                    tile = jnp.where(live[k], held_tiles[a, k, rows, :], 0.0)
                    total = tile if total is None else total + tile
                    for j in range(SWEEPS):
                        held[j][k] = jnp.where(chosen[j] == float(a), tile, held[j][k])
                sums[a, rows, :] = total
            for j in range(SWEEPS):
                for k in range(slots):
                    loads[j][pl.ds(k * width + r, 8), :] = held[j][k]
    inverse = discount / lane_sums(actions, lambda a: sums[a])
    scale[...] = inverse
    at = lax.broadcasted_iota(jnp.int32, (actions, width), 0)
    for j in range(SWEEPS):
        here = at == policy[pl.ds(j, 1), :]
        picked_scale = jnp.sum(jnp.where(here, inverse, 0.0), axis=0, keepdims=True)
        picked_reward = jnp.sum(jnp.where(here, reward[...], 0.0), axis=0, keepdims=True)
        loads[j][pl.ds(slots * width, AUX), :] = stacked([picked_scale, picked_reward] + columns_of, AUX)


def fetched(table, gathered):
    out = []
    for k in range(table.shape[1]):
        at = table[0, k]
        row = gathered[pl.ds(jnp.maximum(at, 0), 1), :]
        out.append(jnp.where(at >= 0, row, 0.0))
    return out


def back_up(table, gathered, reward, scale, tiles, out, sums, *stream):
    actions, slots, width, _ = tiles.shape
    if stream:
        held_tiles, sems = stream
        for g in range(width // CHUNK):
            chunk(g, tiles, held_tiles, sems).start()
    else:
        held_tiles = tiles
    blocks = [jnp.broadcast_to(b, (8, width)) for b in fetched(table, gathered)]
    for g in range(width // CHUNK):
        if stream:
            chunk(g, tiles, held_tiles, sems).wait()
        for r in range(g * CHUNK, (g + 1) * CHUNK, 8):
            rows = pl.ds(r, 8)
            for a in range(actions):
                total = held_tiles[a, 0, rows, :] * blocks[0]
                for k in range(1, slots):
                    total += held_tiles[a, k, rows, :] * blocks[k]
                sums[a, rows, :] = total
    weighted = lane_sums(actions, lambda a: sums[a])
    backup = jnp.max(reward[...] + scale[...] * weighted, axis=0, keepdims=True)
    out[...] = jnp.broadcast_to(backup, out.shape)


def parts(loads, held_loads, sems):
    high = held_loads.shape[0] // sems.shape[0]
    rows = [pl.ds(b * high, high) for b in range(sems.shape[0])]
    return [pltpu.make_async_copy(loads.at[r, :], held_loads.at[r, :], sems.at[b]) for b, r in enumerate(rows)]


def line_product(gathered, loads, arriving):
    states, width = gathered.shape
    high = width * 4 + AUX
    blocks = loads.shape[0] // high
    halves = [pieces(gathered[pl.ds(h * width, width), :], 3) for h in range(states // width)]
    lane = lax.broadcasted_iota(jnp.int32, (16, width), 1).astype(jnp.float32)
    aux = []

    def weighted_rows(b):
        if arriving:
            arriving[b].wait()
        aux.append(loads[pl.ds(b * high + 4 * width, AUX), :])
        named = jnp.concatenate([aux[b], aux[b]], axis=0)
        fetched_rows = jnp.zeros((16, width), jnp.float32)
        for h, cut in enumerate(halves):
            chosen = jnp.where(named == lane + float(h * width), 1.0, 0.0).astype(jnp.bfloat16)
            for piece in cut:
                fetched_rows += jnp.dot(chosen, piece, preferred_element_type=jnp.float32)
        total = None
        for k in range(4):
            term = loads[pl.ds(b * high + k * width, width), :] * fetched_rows[2 + k : 3 + k]
            total = term if total is None else total + term
        return total

    weighted = lane_sums(blocks, weighted_rows)[:blocks]
    scale = stacked([a[0:1] for a in aux], blocks)
    reward = stacked([a[1:2] for a in aux], blocks)
    return reward + scale * weighted


def spread_out(out, got):
    for i in range(out.shape[0] // got.shape[0]):
        out[pl.ds(i * got.shape[0], got.shape[0]), :] = got


def first_evaluation(j, gathered, before, held, loads, out, bounds, held_loads, sems):
    arriving = parts(loads, held_loads, sems)
    for copy in arriving:
        copy.start()
    change = gathered[...] - before[...]
    top = jnp.max(change)
    bottom = jnp.min(change)
    offset = shift * (bottom + top)
    spread_out(out, line_product(gathered, held_loads, arriving) + discount * offset)
    sweep = lax.broadcasted_iota(jnp.int32, bounds.shape, 0)
    side = lax.broadcasted_iota(jnp.int32, bounds.shape, 1)
    bounds[...] = jnp.where(sweep < j, held[...], jnp.where(side == 0, bottom, top))


def next_evaluation(gathered, loads, out, *stream):
    arriving = []
    if stream:
        arriving = parts(loads, *stream)
        for copy in arriving:
            copy.start()
        loads = stream[0]
    spread_out(out, line_product(gathered, loads, arriving))


def last_evaluation(table, gathered, load, held, out, bounds):
    slots, width = table.shape[1], gathered.shape[1]
    blocks = fetched(table, gathered)
    total = load[pl.ds(0, width), :] * blocks[0]
    for k in range(1, slots):
        total += load[pl.ds(k * width, width), :] * blocks[k]
    weighted = lane_sums(1, lambda _: total)[0:1]
    aux = load[pl.ds(slots * width, AUX), :]
    out[...] = aux[1:2] + aux[0:1] * weighted
    bounds[...] = held[...]


SCALARS = pl.BlockSpec(memory_space=pltpu.SMEM)
VECTORS = pl.BlockSpec(memory_space=pltpu.VMEM)
LEFT = pl.BlockSpec(memory_space=pltpu.HBM)


def shaped(*shape):
    return jax.ShapeDtypeStruct(shape, jnp.float32)


def called(body, given, out_shape, name, scratch=(), scalars=0, left=0, limit=8):
    inside = len(given) - scalars - left
    given = given[: scalars + inside] + tuple(pltpu.with_memory_space_constraint(x, pltpu.HBM) for x in given[scalars + inside :])
    return pl.pallas_call(
        body,
        out_shape=out_shape,
        in_specs=[SCALARS] * scalars + [VECTORS] * inside + [LEFT] * left,
        out_specs=jax.tree.map(lambda _: VECTORS, out_shape),
        scratch_shapes=list(scratch),
        compiler_params=pltpu.CompilerParams(vmem_limit_bytes=limit * MIB),
        name=name,
    )(*given)


def over_all(rows):
    return lax.all_to_all(rows, ORDER, 0, 0, tiled=True)


def over_plane(rows):
    return lax.all_to_all(rows, PLANE, 0, 0, tiled=True)


def over_line(load):
    return lax.all_gather(load, LINE, axis=0, tiled=True)


def local(tiles, counts, col_index, reward, policy, start_values):
    actions, _, slots, width, _ = tiles.shape
    devices = lax.axis_size(AXES)
    tiles = tiles.reshape(actions, slots, width, width)
    all_rows = shaped(devices, width)
    load = shaped(slots * width + AUX, width)
    square = pltpu.VMEM((actions, width, width), jnp.float32)
    tiles_scratch = pltpu.VMEM(tiles.shape, jnp.float32)
    chunks = pltpu.SemaphoreType.DMA((width // CHUNK,))
    given = (col_index, start_values.reshape(1, width), policy, reward, tiles)
    rows, table, scale, load_0, load_1 = pl.pallas_call(
        prepare,
        out_shape=(all_rows, jax.ShapeDtypeStruct(col_index.shape, jnp.int32), shaped(actions, width), load, load),
        in_specs=[SCALARS] + [LEFT] * 5,
        out_specs=(VECTORS, SCALARS, VECTORS, VECTORS, VECTORS),
        scratch_shapes=[
            pltpu.SMEM(col_index.shape, jnp.int32),
            pltpu.VMEM((1, width), jnp.float32),
            pltpu.VMEM(policy.shape, jnp.int32),
            pltpu.VMEM(reward.shape, jnp.float32),
            tiles_scratch,
            square,
            pltpu.VMEM((SWEEPS, width, width), jnp.float32),
            chunks,
            pltpu.SemaphoreType.DMA((4,)),
        ],
        compiler_params=pltpu.CompilerParams(vmem_limit_bytes=12 * MIB),
        name="prepare",
    )(counts, *(pltpu.with_memory_space_constraint(x, pltpu.HBM) for x in given))

    line = lax.axis_size(LINE)
    arrivals = pltpu.SemaphoreType.DMA((line,))
    line_rows = line * (slots * width + AUX)
    held_shape = shaped(line_rows, width)
    loads = over_line(load_0)
    gathered = over_all(rows)
    bounds = jnp.zeros((SWEEPS, 2), jnp.float32)
    for j in range(SWEEPS):
        given = (table, gathered, reward, scale, tiles)
        scratch = [square] + [tiles_scratch, chunks] * (j == 0)
        backup = called(back_up, given, all_rows, f"back_up_{j}", scratch, 1, int(j == 0), 12)
        before, gathered = gathered, over_all(backup)
        if j == 0:
            load_1, gathered = lax.optimization_barrier((load_1, gathered))
            later_loads = over_line(load_1)
        body = functools.partial(first_evaluation, j)
        given = (gathered, before, bounds, loads)
        made = (all_rows, shaped(SWEEPS, 2))
        if KEEP and j == 0:
            current, bounds, loads = called(body, given, made + (held_shape,), f"first_evaluation_{j}", [arrivals], 0, 1)
        else:
            scratch = [pltpu.VMEM((line_rows, width), jnp.float32), arrivals]
            current, bounds = called(body, given, made, f"first_evaluation_{j}", scratch, 0, 1)
        gathered = over_plane(current)
        if j < SWEEPS - 1:
            scratch = [] if KEEP else scratch
            current = called(next_evaluation, (gathered, loads), all_rows, f"next_evaluation_{j}", scratch, 0, int(not KEEP))
            gathered = over_plane(current)
            loads = later_loads
    given = (table, gathered, load_1, bounds)
    current, bounds = called(last_evaluation, given, (shaped(1, width), shaped(SWEEPS, 2)), "last_evaluation", (), 1)
    return current.reshape(width), bounds


def solution(mesh):
    split = Mesh(mesh.devices.reshape(4, 4, 8, 2), AXES)
    placed = (
        P(None, AXES, None, None, None),
        P(AXES),
        P(AXES, None),
        P(None, AXES),
        P(None, AXES),
        P(AXES),
    )
    return jax.shard_map(local, mesh=split, in_specs=placed, out_specs=(P(AXES), P()), check_vma=False)
```

```python
import functools

import jax
import jax.numpy as jnp
from jax import lax
from jax.experimental import pallas as pl
from jax.experimental.pallas import tpu as pltpu
from jax.sharding import Mesh
from jax.sharding import PartitionSpec as P

SWEEPS = 2
AXES = ("x", "y", "z", "c")
ORDER = ("y", "z", "c", "x")
PLANE = ("y", "z", "c")
LINE = "x"
discount = 0.9
shift = discount / (1.0 - discount) * 0.5
MIB = 1 << 20
AUX = 8
CHUNK = 32


def pieces(values, count):
    out = []
    for left in reversed(range(count)):
        piece = values.astype(jnp.bfloat16)
        out.append(piece)
        if left:
            values = values - piece.astype(jnp.float32)
    return out


def contract(left, right, dims, count):
    out = None
    for piece in pieces(right, count):
        term = lax.dot_general(left, piece, (dims, ((), ())), preferred_element_type=jnp.float32)
        out = term if out is None else out + term
    return out


def lane_sums(count, row_values, places=None):
    at = lax.broadcasted_iota(jnp.int32, (16, 128), 0)
    out = jnp.zeros((16, 128), jnp.float32)
    for i in range(count):
        row = jnp.where(at == (places[i] if places else i), 1.0, 0.0).astype(jnp.bfloat16)
        out += contract(row, row_values(i), ((1,), (1,)), 2)
    return out


def stacked(rows, height, places=None):
    at = lax.broadcasted_iota(jnp.int32, (height, rows[0].shape[-1]), 0)
    out = jnp.zeros(at.shape, jnp.float32)
    for i, row in enumerate(rows):
        out = jnp.where(at == (places[i] if places else i), row, out)
    return out


def chunk(g, tiles, held_tiles, sems):
    rows = pl.ds(g * CHUNK, CHUNK)
    return pltpu.make_async_copy(tiles.at[:, :, rows, :], held_tiles.at[:, :, rows, :], sems.at[g])


def prepare(
    counts, at, columns_in, policy_in, reward_in, tiles,
    table, scale, load, held_tiles,
    col_index, policy, reward, sums, columns, sems, small_sems,
):
    actions, slots, width, _ = tiles.shape
    high = slots * width + AUX
    given = ((columns_in, col_index), (policy_in, policy), (reward_in, reward))
    small = [pltpu.make_async_copy(source, target, small_sems.at[i]) for i, (source, target) in enumerate(given)]
    for copy in small:
        copy.start()
    for g in range(width // CHUNK):
        chunk(g, tiles, held_tiles, sems).start()
    for copy in small:
        copy.wait()
    table[0, slots] = at[0, 0]
    columns_of = []
    for k in range(slots):
        block = col_index[0, k]
        place = (block % 64) * 4 + block // 64
        place = jnp.where(counts[0] > k, place, -1)
        table[0, k] = place
        columns_of.append(jnp.full((1, width), place.astype(jnp.float32)))
    live = [counts[0] > k for k in range(slots)]
    for j in range(SWEEPS):
        columns[j] = jnp.broadcast_to(policy[pl.ds(j, 1), :].astype(jnp.float32), (width, width)).T
    for g in range(width // CHUNK):
        chunk(g, tiles, held_tiles, sems).wait()
        for r in range(g * CHUNK, (g + 1) * CHUNK, 8):
            rows = pl.ds(r, 8)
            chosen = [columns[j, rows, :] for j in range(SWEEPS)]
            held = [[jnp.zeros((8, width), jnp.float32) for _ in range(slots)] for _ in range(SWEEPS)]
            for a in range(actions):
                total = None
                for k in range(slots):
                    tile = jnp.where(live[k], held_tiles[a, k, rows, :], 0.0)
                    total = tile if total is None else total + tile
                    for j in range(SWEEPS):
                        held[j][k] = jnp.where(chosen[j] == float(a), tile, held[j][k])
                sums[a, rows, :] = total
            for j in range(SWEEPS):
                for k in range(slots):
                    load[pl.ds(j * high + k * width + r, 8), :] = held[j][k]
    inverse = discount / lane_sums(actions, lambda a: sums[a])
    scale[...] = inverse
    at = lax.broadcasted_iota(jnp.int32, (actions, width), 0)
    for j in range(SWEEPS):
        here = at == policy[pl.ds(j, 1), :]
        picked_scale = jnp.sum(jnp.where(here, inverse, 0.0), axis=0, keepdims=True)
        picked_reward = jnp.sum(jnp.where(here, reward[...], 0.0), axis=0, keepdims=True)
        load[pl.ds(j * high + slots * width, AUX), :] = stacked([picked_scale, picked_reward] + columns_of, AUX)


def fetched(table, gathered):
    out = []
    for k in range(table.shape[1] - 1):
        at = table[0, k]
        row = gathered[pl.ds(jnp.maximum(at, 0), 1), :]
        out.append(jnp.where(at >= 0, row, 0.0))
    return out


def back_up(table, gathered, tiles, reward, scale, out, sums):
    actions, slots, width, _ = tiles.shape
    blocks = [jnp.broadcast_to(b, (8, width)) for b in fetched(table, gathered)]
    for r in range(0, width, 8):
        rows = pl.ds(r, 8)
        for a in range(actions):
            total = tiles[a, 0, rows, :] * blocks[0]
            for k in range(1, slots):
                total += tiles[a, k, rows, :] * blocks[k]
            sums[a, rows, :] = total
    weighted = lane_sums(actions, lambda a: sums[a])
    backup = jnp.max(reward[...] + scale[...] * weighted, axis=0, keepdims=True)
    out[...] = jnp.broadcast_to(backup, out.shape)


def line_product(j, at, gathered, loads):
    states, width = gathered.shape
    slots, count = 4, len(loads)
    first = j * (slots * width + AUX)
    aux = [load[pl.ds(first + slots * width, AUX), :] for load in loads]
    named = jnp.concatenate(aux, axis=0)
    lane = lax.broadcasted_iota(jnp.int32, named.shape, 1).astype(jnp.float32)
    fetched_rows = None
    for h in range(states // width):
        chosen = jnp.where(named == lane + float(h * width), 1.0, 0.0).astype(jnp.bfloat16)
        term = contract(chosen, gathered[pl.ds(h * width, width), :], ((1,), (0,)), 3)
        fetched_rows = term if fetched_rows is None else fetched_rows + term

    def weighted_rows(b):
        total = None
        for k in range(slots):
            row = b * AUX + 2 + k
            term = loads[b][pl.ds(first + k * width, width), :] * fetched_rows[row : row + 1]
            total = term if total is None else total + term
        return total

    owners = [lax.rem(at - b + count, count) for b in range(count)]
    weighted = lane_sums(count, weighted_rows, owners)[:8]
    scale = stacked([a[0:1] for a in aux], 8, owners)
    reward = stacked([a[1:2] for a in aux], 8, owners)
    return (reward + scale * weighted)[:count]


def spread_out(out, got):
    got = jnp.concatenate([got] * (8 // got.shape[0]), axis=0)
    for i in range(out.shape[0] // 8):
        out[pl.ds(i * 8, 8), :] = got


def first_evaluation(j, table, gathered, before, held, *refs):
    *loads, out, bounds = refs
    change = gathered[...] - before[...]
    top = jnp.max(change)
    bottom = jnp.min(change)
    offset = shift * (bottom + top)
    spread_out(out, line_product(j, table[0, table.shape[1] - 1], gathered, loads) + discount * offset)
    sweep = lax.broadcasted_iota(jnp.int32, bounds.shape, 0)
    side = lax.broadcasted_iota(jnp.int32, bounds.shape, 1)
    bounds[...] = jnp.where(sweep < j, held[...], jnp.where(side == 0, bottom, top))


def next_evaluation(j, table, gathered, *refs):
    *loads, out = refs
    spread_out(out, line_product(j, table[0, table.shape[1] - 1], gathered, loads))


def last_evaluation(j, table, gathered, load, held, out, bounds):
    slots, width = table.shape[1] - 1, gathered.shape[1]
    first = j * (slots * width + AUX)
    blocks = fetched(table, gathered)
    total = load[pl.ds(first, width), :] * blocks[0]
    for k in range(1, slots):
        total += load[pl.ds(first + k * width, width), :] * blocks[k]
    weighted = lane_sums(1, lambda _: total)[0:1]
    aux = load[pl.ds(first + slots * width, AUX), :]
    out[...] = aux[1:2] + aux[0:1] * weighted
    bounds[...] = held[...]


SCALARS = pl.BlockSpec(memory_space=pltpu.SMEM)
VECTORS = pl.BlockSpec(memory_space=pltpu.VMEM)
LEFT = pl.BlockSpec(memory_space=pltpu.HBM)


def shaped(*shape):
    return jax.ShapeDtypeStruct(shape, jnp.float32)


def called(body, given, out_shape, name, scratch=(), limit=8):
    return pl.pallas_call(
        body,
        out_shape=out_shape,
        in_specs=[SCALARS] + [VECTORS] * (len(given) - 1),
        out_specs=jax.tree.map(lambda _: VECTORS, out_shape),
        scratch_shapes=list(scratch),
        compiler_params=pltpu.CompilerParams(vmem_limit_bytes=limit * MIB),
        name=name,
    )(*given)


def over_all(rows):
    return lax.all_to_all(rows, ORDER, 0, 0, tiled=True)


def over_plane(rows):
    return lax.all_to_all(rows, PLANE, 0, 0, tiled=True)


def local(tiles, counts, col_index, reward, policy, start_values):
    actions, _, slots, width, _ = tiles.shape
    devices, line = lax.axis_size(AXES), lax.axis_size(LINE)
    tiles = tiles.reshape(actions, slots, width, width)
    all_rows = shaped(devices, width)
    square = pltpu.VMEM((actions, width, width), jnp.float32)
    gathered = over_all(jnp.broadcast_to(start_values[None], (devices, width)))
    given = (col_index, policy, reward, tiles)
    table, scale, load, held_tiles = pl.pallas_call(
        prepare,
        out_shape=(
            jax.ShapeDtypeStruct((1, slots + 1), jnp.int32),
            shaped(actions, width),
            shaped(SWEEPS * (slots * width + AUX), width),
            shaped(*tiles.shape),
        ),
        in_specs=[SCALARS] * 2 + [LEFT] * 4,
        out_specs=(SCALARS, VECTORS, VECTORS, VECTORS),
        scratch_shapes=[
            pltpu.SMEM(col_index.shape, jnp.int32),
            pltpu.VMEM(policy.shape, jnp.int32),
            pltpu.VMEM(reward.shape, jnp.float32),
            square,
            pltpu.VMEM((SWEEPS, width, width), jnp.float32),
            pltpu.SemaphoreType.DMA((width // CHUNK,)),
            pltpu.SemaphoreType.DMA((3,)),
        ],
        compiler_params=pltpu.CompilerParams(vmem_limit_bytes=8 * MIB),
        name="prepare",
            cost_estimate=pl.CostEstimate(flops=4_000_000, bytes_accessed=8_000_000, transcendentals=0),
    )(counts, lax.axis_index(LINE).reshape(1, 1), *(pltpu.with_memory_space_constraint(x, pltpu.HBM) for x in given))
    loads = [load] + [lax.ppermute(load, LINE, [(i, (i + k) % line) for i in range(line)]) for k in range(1, line)]

    bounds = jnp.zeros((SWEEPS, 2), jnp.float32)
    for j in range(SWEEPS):
        backup = called(back_up, (table, gathered, held_tiles, reward, scale), all_rows, f"back_up_{j}", [square])
        before, gathered = gathered, over_all(backup)
        body = functools.partial(first_evaluation, j)
        made = (all_rows, shaped(SWEEPS, 2))
        current, bounds = called(body, (table, gathered, before, bounds, *loads), made, f"first_evaluation_{j}")
        gathered = over_plane(current)
        if j < SWEEPS - 1:
            current = called(functools.partial(next_evaluation, j), (table, gathered, *loads), all_rows, f"next_evaluation_{j}")
            gathered = over_plane(current)
    body = functools.partial(last_evaluation, SWEEPS - 1)
    current, bounds = called(body, (table, gathered, load, bounds), (shaped(1, width), shaped(SWEEPS, 2)), "last_evaluation")
    return current.reshape(width), bounds


def solution(mesh):
    split = Mesh(mesh.devices.reshape(4, 4, 8, 2), AXES)
    placed = (
        P(None, AXES, None, None, None),
        P(AXES),
        P(AXES, None),
        P(None, AXES),
        P(None, AXES),
        P(AXES),
    )
    return jax.shard_map(local, mesh=split, in_specs=placed, out_specs=(P(AXES), P()), check_vma=False)
```

```python
import functools

import jax
import jax.numpy as jnp
from jax import lax
from jax.experimental import pallas as pl
from jax.experimental.pallas import tpu as pltpu
from jax.sharding import Mesh
from jax.sharding import PartitionSpec as P

SWEEPS = 2
AXES = ("x", "y", "z", "c")
discount = 0.9
shift = discount / (1.0 - discount) * 0.5
MIB = 1 << 20
AUX = 8
CHUNK = 32
KEPT = 10


def pieces(values, count):
    out = []
    for left in reversed(range(count)):
        piece = values.astype(jnp.bfloat16)
        out.append(piece)
        if left:
            values = values - piece.astype(jnp.float32)
    return out


def lane_sums(count, row_values):
    at = lax.broadcasted_iota(jnp.int32, (16, 128), 0)
    out = jnp.zeros((16, 128), jnp.float32)
    for i in range(count):
        row = jnp.where(at == i, 1.0, 0.0).astype(jnp.bfloat16)
        for piece in pieces(row_values(i), 2):
            out += lax.dot_general(row, piece, (((1,), (1,)), ((), ())), preferred_element_type=jnp.float32)
    return out


def stacked(rows, height):
    at = lax.broadcasted_iota(jnp.int32, (height, rows[0].shape[-1]), 0)
    out = jnp.zeros(at.shape, jnp.float32)
    for i, row in enumerate(rows):
        out = jnp.where(at == i, row, out)
    return out


def chunk(g, tiles, kept, others, sems):
    rows = pl.ds(g * CHUNK, CHUNK)
    return [
        pltpu.make_async_copy(tiles.at[pl.ds(0, KEPT), :, rows, :], kept.at[:, :, rows, :], sems.at[g, 0]),
        pltpu.make_async_copy(tiles.at[pl.ds(KEPT, others.shape[0]), :, rows, :], others.at[:, :, rows, :], sems.at[g, 1]),
    ]


def prepare(
    counts, columns_in, policy_in, reward_in, tiles,
    table, scale, load, kept,
    col_index, policy, reward, others, sums, columns, sems, small_sems,
):
    actions, slots, width, _ = tiles.shape
    high = slots * width + AUX
    given = ((columns_in, col_index), (policy_in, policy), (reward_in, reward))
    small = [pltpu.make_async_copy(source, target, small_sems.at[i]) for i, (source, target) in enumerate(given)]
    for copy in small:
        copy.start()
    for g in range(width // CHUNK):
        for copy in chunk(g, tiles, kept, others, sems):
            copy.start()
    for copy in small:
        copy.wait()
    for k in range(slots):
        table[0, k] = jnp.where(counts[0] > k, col_index[0, k], -1)
    live = [counts[0] > k for k in range(slots)]
    for j in range(SWEEPS):
        columns[j] = jnp.broadcast_to(policy[pl.ds(j, 1), :].astype(jnp.float32), (width, width)).T
    for g in range(width // CHUNK):
        for copy in chunk(g, tiles, kept, others, sems):
            copy.wait()
        for r in range(g * CHUNK, (g + 1) * CHUNK, 8):
            rows = pl.ds(r, 8)
            chosen = [columns[j, rows, :] for j in range(SWEEPS)]
            held = [[jnp.zeros((8, width), jnp.float32) for _ in range(slots)] for _ in range(SWEEPS)]
            for a in range(actions):
                total = None
                for k in range(slots):
                    source, place = (kept, a) if a < KEPT else (others, a - KEPT)
                    tile = jnp.where(live[k], source[place, k, rows, :], 0.0)
                    total = tile if total is None else total + tile
                    for j in range(SWEEPS):
                        held[j][k] = jnp.where(chosen[j] == float(a), tile, held[j][k])
                sums[a, rows, :] = total
            for j in range(SWEEPS):
                for k in range(slots):
                    load[pl.ds(j * high + k * width + r, 8), :] = held[j][k]
    inverse = discount / lane_sums(actions, lambda a: sums[a])
    scale[...] = inverse
    at = lax.broadcasted_iota(jnp.int32, (actions, width), 0)
    for j in range(SWEEPS):
        here = at == policy[pl.ds(j, 1), :]
        picked_scale = jnp.sum(jnp.where(here, inverse, 0.0), axis=0, keepdims=True)
        picked_reward = jnp.sum(jnp.where(here, reward[...], 0.0), axis=0, keepdims=True)
        load[pl.ds(j * high + slots * width, AUX), :] = stacked([picked_scale, picked_reward], AUX)


def fetched(table, gathered):
    out = []
    for k in range(table.shape[1]):
        at = table[0, k]
        row = gathered[pl.ds(jnp.maximum(at, 0), 1), :]
        out.append(jnp.where(at >= 0, row, 0.0))
    return out


def back_up(table, gathered, *refs):
    if len(refs) == 5:
        tiles, reward, scale, out, sums = refs
        arriving = []
    else:
        kept, reward, scale, source, out, sums, others, sems = refs
        ends = [pltpu.make_async_copy(source.at[KEPT + i], others.at[i], sems.at[i]) for i in range(others.shape[0])]
        arriving = [None] * KEPT + ends
        for copy in ends:
            copy.start()
    actions, width, _ = sums.shape
    blocks = [jnp.broadcast_to(b, (8, width)) for b in fetched(table, gathered)]
    for a in range(actions):
        held, place = (tiles, a) if not arriving else (kept, a) if a < KEPT else (others, a - KEPT)
        if arriving and arriving[a]:
            arriving[a].wait()
        for r in range(0, width, 8):
            rows = pl.ds(r, 8)
            total = held[place, 0, rows, :] * blocks[0]
            for k in range(1, len(blocks)):
                total += held[place, k, rows, :] * blocks[k]
            sums[a, rows, :] = total
    weighted = lane_sums(actions, lambda a: sums[a])
    backup = jnp.max(reward[...] + scale[...] * weighted, axis=0, keepdims=True)
    out[...] = jnp.broadcast_to(backup, out.shape)


def evaluated(j, table, gathered, load):
    slots, width = table.shape[1], gathered.shape[1]
    first = j * (slots * width + AUX)
    blocks = fetched(table, gathered)
    total = load[pl.ds(first, width), :] * blocks[0]
    for k in range(1, slots):
        total += load[pl.ds(first + k * width, width), :] * blocks[k]
    weighted = lane_sums(1, lambda _: total)[0:1]
    aux = load[pl.ds(first + slots * width, AUX), :]
    return aux[1:2] + aux[0:1] * weighted


def first_evaluation(j, table, gathered, before, held, load, out, bounds):
    change = gathered[...] - before[...]
    top = jnp.max(change)
    bottom = jnp.min(change)
    offset = shift * (bottom + top)
    out[...] = jnp.broadcast_to(evaluated(j, table, gathered, load) + discount * offset, out.shape)
    sweep = lax.broadcasted_iota(jnp.int32, bounds.shape, 0)
    side = lax.broadcasted_iota(jnp.int32, bounds.shape, 1)
    bounds[...] = jnp.where(sweep < j, held[...], jnp.where(side == 0, bottom, top))


def next_evaluation(j, table, gathered, load, out):
    out[...] = jnp.broadcast_to(evaluated(j, table, gathered, load), out.shape)


def last_evaluation(j, table, gathered, load, held, out, bounds):
    out[...] = evaluated(j, table, gathered, load)
    bounds[...] = held[...]


SCALARS = pl.BlockSpec(memory_space=pltpu.SMEM)
VECTORS = pl.BlockSpec(memory_space=pltpu.VMEM)
LEFT = pl.BlockSpec(memory_space=pltpu.HBM)


def shaped(*shape):
    return jax.ShapeDtypeStruct(shape, jnp.float32)


def called(body, given, out_shape, name, scratch=(), limit=8, left=0):
    return pl.pallas_call(
        body,
        out_shape=out_shape,
        in_specs=[SCALARS] + [VECTORS] * (len(given) - 1 - left) + [LEFT] * left,
        out_specs=jax.tree.map(lambda _: VECTORS, out_shape),
        scratch_shapes=list(scratch),
        compiler_params=pltpu.CompilerParams(vmem_limit_bytes=limit * MIB),
        name=name,
    )(*given)


def exchange(rows):
    return lax.all_to_all(rows, AXES, 0, 0, tiled=True)


def local(tiles, counts, col_index, reward, policy, start_values):
    actions, _, slots, width, _ = tiles.shape
    devices = lax.axis_size(AXES)
    tiles = tiles.reshape(actions, slots, width, width)
    all_rows = shaped(devices, width)
    square = pltpu.VMEM((actions, width, width), jnp.float32)
    gathered = exchange(jnp.broadcast_to(start_values[None], (devices, width)))
    given = (col_index, policy, reward, tiles)
    table, scale, load, kept = pl.pallas_call(
        prepare,
        out_shape=(
            jax.ShapeDtypeStruct(col_index.shape, jnp.int32),
            shaped(actions, width),
            shaped(SWEEPS * (slots * width + AUX), width),
            shaped(KEPT, *tiles.shape[1:]),
        ),
        in_specs=[SCALARS] + [LEFT] * 4,
        out_specs=(SCALARS, VECTORS, VECTORS, VECTORS),
        scratch_shapes=[
            pltpu.SMEM(col_index.shape, jnp.int32),
            pltpu.VMEM(policy.shape, jnp.int32),
            pltpu.VMEM(reward.shape, jnp.float32),
            pltpu.VMEM((actions - KEPT, *tiles.shape[1:]), jnp.float32),
            square,
            pltpu.VMEM((SWEEPS, width, width), jnp.float32),
            pltpu.SemaphoreType.DMA((width // CHUNK, 2)),
            pltpu.SemaphoreType.DMA((3,)),
        ],
        compiler_params=pltpu.CompilerParams(vmem_limit_bytes=8 * MIB),
        name="prepare",
            cost_estimate=pl.CostEstimate(flops=4_000_000, bytes_accessed=8_000_000, transcendentals=0),
    )(counts, *(pltpu.with_memory_space_constraint(x, pltpu.HBM) for x in given))
    bounds = jnp.zeros((SWEEPS, 2), jnp.float32)
    for j in range(SWEEPS):
        if j == 0:
            source = pltpu.with_memory_space_constraint(tiles, pltpu.HBM)
            rest = [pltpu.VMEM((actions - KEPT, *tiles.shape[1:]), jnp.float32), pltpu.SemaphoreType.DMA((actions - KEPT,))]
            given = (table, gathered, kept, reward, scale, source)
            backup = called(back_up, given, all_rows, f"back_up_{j}", [square] + rest, left=1)
        else:
            backup = called(back_up, (table, gathered, tiles, reward, scale), all_rows, f"back_up_{j}", [square])
        before, gathered = gathered, exchange(backup)
        if j == 0:
            tiles, gathered = lax.optimization_barrier((tiles, gathered))
        body = functools.partial(first_evaluation, j)
        made = (all_rows, shaped(SWEEPS, 2))
        current, bounds = called(body, (table, gathered, before, bounds, load), made, f"first_evaluation_{j}")
        gathered = exchange(current)
        if j < SWEEPS - 1:
            current = called(functools.partial(next_evaluation, j), (table, gathered, load), all_rows, f"next_evaluation_{j}")
            gathered = exchange(current)
    body = functools.partial(last_evaluation, SWEEPS - 1)
    current, bounds = called(body, (table, gathered, load, bounds), (shaped(1, width), shaped(SWEEPS, 2)), "last_evaluation")
    return current.reshape(width), bounds


def solution(mesh):
    split = Mesh(mesh.devices.reshape(4, 4, 8, 2), AXES)
    placed = (
        P(None, AXES, None, None, None),
        P(AXES),
        P(AXES, None),
        P(None, AXES),
        P(None, AXES),
        P(AXES),
    )
    return jax.shard_map(local, mesh=split, in_specs=placed, out_specs=(P(AXES), P()), check_vma=False)
```

```python
import functools

import jax
import jax.numpy as jnp
from jax import lax
from jax.experimental import pallas as pl
from jax.experimental.pallas import tpu as pltpu
from jax.sharding import Mesh
from jax.sharding import PartitionSpec as P

SWEEPS = 2
AXES = ("x", "y", "z", "c")
discount = 0.9
shift = discount / (1.0 - discount) * 0.5
MIB = 1 << 20
AUX = 8
CHUNK = 32
KEPT = 10


def pieces(values, count):
    out = []
    for left in reversed(range(count)):
        piece = values.astype(jnp.bfloat16)
        out.append(piece)
        if left:
            values = values - piece.astype(jnp.float32)
    return out


def lane_sums(count, row_values):
    at = lax.broadcasted_iota(jnp.int32, (16, 128), 0)
    out = jnp.zeros((16, 128), jnp.float32)
    for i in range(count):
        row = jnp.where(at == i, 1.0, 0.0).astype(jnp.bfloat16)
        for piece in pieces(row_values(i), 2):
            out += lax.dot_general(row, piece, (((1,), (1,)), ((), ())), preferred_element_type=jnp.float32)
    return out


def stacked(rows, height):
    at = lax.broadcasted_iota(jnp.int32, (height, rows[0].shape[-1]), 0)
    out = jnp.zeros(at.shape, jnp.float32)
    for i, row in enumerate(rows):
        out = jnp.where(at == i, row, out)
    return out


def chunk(g, tiles, kept, others, sems):
    rows = pl.ds(g * CHUNK, CHUNK)
    return [
        pltpu.make_async_copy(tiles.at[pl.ds(0, KEPT), :, rows, :], kept.at[:, :, rows, :], sems.at[g, 0]),
        pltpu.make_async_copy(tiles.at[pl.ds(KEPT, others.shape[0]), :, rows, :], others.at[:, :, rows, :], sems.at[g, 1]),
    ]


def prepare(
    counts, columns_in, policy_in, reward_in, tiles,
    table, scale, load, kept,
    col_index, policy, reward, others, sums, columns, sems, small_sems,
):
    actions, slots, width, _ = tiles.shape
    high = slots * width + AUX
    given = ((columns_in, col_index), (policy_in, policy), (reward_in, reward))
    small = [pltpu.make_async_copy(source, target, small_sems.at[i]) for i, (source, target) in enumerate(given)]
    for copy in small:
        copy.start()
    for g in range(width // CHUNK):
        for copy in chunk(g, tiles, kept, others, sems):
            copy.start()
    for copy in small:
        copy.wait()
    for k in range(slots):
        table[0, k] = jnp.where(counts[0] > k, col_index[0, k], -1)
    live = [counts[0] > k for k in range(slots)]
    for j in range(SWEEPS):
        columns[j] = jnp.broadcast_to(policy[pl.ds(j, 1), :].astype(jnp.float32), (width, width)).T
    for g in range(width // CHUNK):
        for copy in chunk(g, tiles, kept, others, sems):
            copy.wait()
        for r in range(g * CHUNK, (g + 1) * CHUNK, 8):
            rows = pl.ds(r, 8)
            chosen = [columns[j, rows, :] for j in range(SWEEPS)]
            held = [[jnp.zeros((8, width), jnp.float32) for _ in range(slots)] for _ in range(SWEEPS)]
            for a in range(actions):
                total = None
                for k in range(slots):
                    source, place = (kept, a) if a < KEPT else (others, a - KEPT)
                    tile = jnp.where(live[k], source[place, k, rows, :], 0.0)
                    total = tile if total is None else total + tile
                    for j in range(SWEEPS):
                        held[j][k] = jnp.where(chosen[j] == float(a), tile, held[j][k])
                sums[a, rows, :] = total
            for j in range(SWEEPS):
                for k in range(slots):
                    load[pl.ds(j * high + k * width + r, 8), :] = held[j][k]
    inverse = discount / lane_sums(actions, lambda a: sums[a])
    scale[...] = inverse
    at = lax.broadcasted_iota(jnp.int32, (actions, width), 0)
    for j in range(SWEEPS):
        here = at == policy[pl.ds(j, 1), :]
        picked_scale = jnp.sum(jnp.where(here, inverse, 0.0), axis=0, keepdims=True)
        picked_reward = jnp.sum(jnp.where(here, reward[...], 0.0), axis=0, keepdims=True)
        load[pl.ds(j * high + slots * width, AUX), :] = stacked([picked_scale, picked_reward], AUX)


def fetched(table, gathered):
    out = []
    for k in range(table.shape[1]):
        at = table[0, k]
        row = gathered[pl.ds(jnp.maximum(at, 0), 1), :]
        out.append(jnp.where(at >= 0, row, 0.0))
    return out


def back_up(table, gathered, kept, reward, scale, source, out, *refs):
    if len(refs) == 3:
        others, sums, sems = refs
        ends = [pltpu.make_async_copy(source.at[KEPT + i], others.at[i], sems.at[i]) for i in range(others.shape[0])]
        for copy in ends:
            copy.start()
    else:
        others, ends = source, []
        (sums,) = refs
    actions, width, _ = sums.shape
    blocks = [jnp.broadcast_to(b, (8, width)) for b in fetched(table, gathered)]
    for a in range(actions):
        held, place = (kept, a) if a < KEPT else (others, a - KEPT)
        if ends and a >= KEPT:
            ends[place].wait()
        for r in range(0, width, 8):
            rows = pl.ds(r, 8)
            total = held[place, 0, rows, :] * blocks[0]
            for k in range(1, len(blocks)):
                total += held[place, k, rows, :] * blocks[k]
            sums[a, rows, :] = total
    weighted = lane_sums(actions, lambda a: sums[a])
    backup = jnp.max(reward[...] + scale[...] * weighted, axis=0, keepdims=True)
    out[...] = jnp.broadcast_to(backup, out.shape)


def evaluated(j, table, gathered, load):
    slots, width = table.shape[1], gathered.shape[1]
    first = j * (slots * width + AUX)
    blocks = fetched(table, gathered)
    total = load[pl.ds(first, width), :] * blocks[0]
    for k in range(1, slots):
        total += load[pl.ds(first + k * width, width), :] * blocks[k]
    weighted = lane_sums(1, lambda _: total)[0:1]
    aux = load[pl.ds(first + slots * width, AUX), :]
    return aux[1:2] + aux[0:1] * weighted


def first_evaluation(j, table, gathered, before, held, load, out, bounds):
    change = gathered[...] - before[...]
    top = jnp.max(change)
    bottom = jnp.min(change)
    offset = shift * (bottom + top)
    out[...] = jnp.broadcast_to(evaluated(j, table, gathered, load) + discount * offset, out.shape)
    sweep = lax.broadcasted_iota(jnp.int32, bounds.shape, 0)
    side = lax.broadcasted_iota(jnp.int32, bounds.shape, 1)
    bounds[...] = jnp.where(sweep < j, held[...], jnp.where(side == 0, bottom, top))


def next_evaluation(j, table, gathered, load, out):
    out[...] = jnp.broadcast_to(evaluated(j, table, gathered, load), out.shape)


def last_evaluation(j, table, gathered, load, held, out, bounds):
    out[...] = evaluated(j, table, gathered, load)
    bounds[...] = held[...]


SCALARS = pl.BlockSpec(memory_space=pltpu.SMEM)
VECTORS = pl.BlockSpec(memory_space=pltpu.VMEM)
LEFT = pl.BlockSpec(memory_space=pltpu.HBM)


def shaped(*shape):
    return jax.ShapeDtypeStruct(shape, jnp.float32)


def called(body, given, out_shape, name, scratch=(), limit=8, left=0):
    return pl.pallas_call(
        body,
        out_shape=out_shape,
        in_specs=[SCALARS] + [VECTORS] * (len(given) - 1 - left) + [LEFT] * left,
        out_specs=jax.tree.map(lambda _: VECTORS, out_shape),
        scratch_shapes=list(scratch),
        compiler_params=pltpu.CompilerParams(vmem_limit_bytes=limit * MIB),
        name=name,
    )(*given)


def exchange(rows):
    return lax.all_to_all(rows, AXES, 0, 0, tiled=True)


def local(tiles, counts, col_index, reward, policy, start_values):
    actions, _, slots, width, _ = tiles.shape
    devices = lax.axis_size(AXES)
    tiles = tiles.reshape(actions, slots, width, width)
    all_rows = shaped(devices, width)
    square = pltpu.VMEM((actions, width, width), jnp.float32)
    gathered = exchange(jnp.broadcast_to(start_values[None], (devices, width)))
    given = (col_index, policy, reward, tiles)
    table, scale, load, kept = pl.pallas_call(
        prepare,
        out_shape=(
            jax.ShapeDtypeStruct(col_index.shape, jnp.int32),
            shaped(actions, width),
            shaped(SWEEPS * (slots * width + AUX), width),
            shaped(KEPT, *tiles.shape[1:]),
        ),
        in_specs=[SCALARS] + [LEFT] * 4,
        out_specs=(SCALARS, VECTORS, VECTORS, VECTORS),
        scratch_shapes=[
            pltpu.SMEM(col_index.shape, jnp.int32),
            pltpu.VMEM(policy.shape, jnp.int32),
            pltpu.VMEM(reward.shape, jnp.float32),
            pltpu.VMEM((actions - KEPT, *tiles.shape[1:]), jnp.float32),
            square,
            pltpu.VMEM((SWEEPS, width, width), jnp.float32),
            pltpu.SemaphoreType.DMA((width // CHUNK, 2)),
            pltpu.SemaphoreType.DMA((3,)),
        ],
        compiler_params=pltpu.CompilerParams(vmem_limit_bytes=8 * MIB),
        name="prepare",
            cost_estimate=pl.CostEstimate(flops=4_000_000, bytes_accessed=8_000_000, transcendentals=0),
    )(counts, *(pltpu.with_memory_space_constraint(x, pltpu.HBM) for x in given))
    bounds = jnp.zeros((SWEEPS, 2), jnp.float32)
    for j in range(SWEEPS):
        if j == 0:
            source = pltpu.with_memory_space_constraint(tiles, pltpu.HBM)
            rest = shaped(actions - KEPT, *tiles.shape[1:])
            given = (table, gathered, kept, reward, scale, source)
            scratch = [square, pltpu.SemaphoreType.DMA((actions - KEPT,))]
            backup, others = called(back_up, given, (all_rows, rest), f"back_up_{j}", scratch, left=1)
        else:
            backup = called(back_up, (table, gathered, kept, reward, scale, others), all_rows, f"back_up_{j}", [square])
        before, gathered = gathered, exchange(backup)
        body = functools.partial(first_evaluation, j)
        made = (all_rows, shaped(SWEEPS, 2))
        current, bounds = called(body, (table, gathered, before, bounds, load), made, f"first_evaluation_{j}")
        gathered = exchange(current)
        if j < SWEEPS - 1:
            current = called(functools.partial(next_evaluation, j), (table, gathered, load), all_rows, f"next_evaluation_{j}")
            gathered = exchange(current)
    body = functools.partial(last_evaluation, SWEEPS - 1)
    current, bounds = called(body, (table, gathered, load, bounds), (shaped(1, width), shaped(SWEEPS, 2)), "last_evaluation")
    return current.reshape(width), bounds


def solution(mesh):
    split = Mesh(mesh.devices.reshape(4, 4, 8, 2), AXES)
    placed = (
        P(None, AXES, None, None, None),
        P(AXES),
        P(AXES, None),
        P(None, AXES),
        P(None, AXES),
        P(AXES),
    )
    return jax.shard_map(local, mesh=split, in_specs=placed, out_specs=(P(AXES), P()), check_vma=False)
```

```python
import functools

import jax
import jax.numpy as jnp
from jax import lax
from jax.experimental import pallas as pl
from jax.experimental.pallas import tpu as pltpu
from jax.sharding import Mesh
from jax.sharding import PartitionSpec as P

SWEEPS = 2
AXES = ("x", "y", "z", "c")
discount = 0.9
shift = discount / (1.0 - discount) * 0.5
MIB = 1 << 20
AUX = 8
CHUNKS = ((0, 32), (32, 32), (64, 32), (96, 24), (120, 8))
KEPT = 10


def pieces(values, count):
    out = []
    for left in reversed(range(count)):
        piece = values.astype(jnp.bfloat16)
        out.append(piece)
        if left:
            values = values - piece.astype(jnp.float32)
    return out


def lane_sums(first, row_values):
    at = lax.broadcasted_iota(jnp.int32, (16, 256), 0)
    out = jnp.zeros((16, 128), jnp.float32)
    for i, values in enumerate(row_values):
        row = jnp.where(at == first + i, 1.0, 0.0).astype(jnp.bfloat16)
        both = jnp.concatenate(pieces(values, 2), axis=1)
        out += lax.dot_general(row, both, (((1,), (1,)), ((), ())), preferred_element_type=jnp.float32)
    return out


def stacked(rows, height):
    at = lax.broadcasted_iota(jnp.int32, (height, rows[0].shape[-1]), 0)
    out = jnp.zeros(at.shape, jnp.float32)
    for i, row in enumerate(rows):
        out = jnp.where(at == i, row, out)
    return out


def chunk(g, tiles, kept, others, sems):
    rows = pl.ds(*CHUNKS[g])
    return [
        pltpu.make_async_copy(tiles.at[pl.ds(0, KEPT), :, rows, :], kept.at[:, :, rows, :], sems.at[g, 0]),
        pltpu.make_async_copy(tiles.at[pl.ds(KEPT, others.shape[0]), :, rows, :], others.at[:, :, rows, :], sems.at[g, 1]),
    ]


def prepare(
    counts, columns_in, policy_in, reward_in, tiles,
    table, scale, load, kept,
    col_index, policy, reward, others, sums, columns, sems, small_sems,
):
    actions, slots, width, _ = tiles.shape
    high = slots * width + AUX
    given = ((columns_in, col_index), (policy_in, policy), (reward_in, reward))
    small = [pltpu.make_async_copy(source, target, small_sems.at[i]) for i, (source, target) in enumerate(given)]
    for copy in small:
        copy.start()
    for g in range(len(CHUNKS)):
        for copy in chunk(g, tiles, kept, others, sems):
            copy.start()
    for copy in small:
        copy.wait()
    for k in range(slots):
        table[0, k] = jnp.where(counts[0] > k, col_index[0, k], -1)
    live = [counts[0] > k for k in range(slots)]
    for j in range(SWEEPS):
        columns[j] = jnp.broadcast_to(policy[pl.ds(j, 1), :].astype(jnp.float32), (width, width)).T
    for g in range(len(CHUNKS)):
        for copy in chunk(g, tiles, kept, others, sems):
            copy.wait()
        for r in range(CHUNKS[g][0], sum(CHUNKS[g]), 8):
            rows = pl.ds(r, 8)
            chosen = [columns[j, rows, :] for j in range(SWEEPS)]
            held = [[jnp.zeros((8, width), jnp.float32) for _ in range(slots)] for _ in range(SWEEPS)]
            for a in range(actions):
                total = None
                for k in range(slots):
                    source, place = (kept, a) if a < KEPT else (others, a - KEPT)
                    tile = jnp.where(live[k], source[place, k, rows, :], 0.0)
                    total = tile if total is None else total + tile
                    for j in range(SWEEPS):
                        held[j][k] = jnp.where(chosen[j] == float(a), tile, held[j][k])
                sums[a, rows, :] = total
            for j in range(SWEEPS):
                for k in range(slots):
                    load[pl.ds(j * high + k * width + r, 8), :] = held[j][k]
    inverse = discount / lane_sums(0, [sums[a] for a in range(actions)])
    scale[...] = inverse
    at = lax.broadcasted_iota(jnp.int32, (actions, width), 0)
    for j in range(SWEEPS):
        here = at == policy[pl.ds(j, 1), :]
        picked_scale = jnp.sum(jnp.where(here, inverse, 0.0), axis=0, keepdims=True)
        picked_reward = jnp.sum(jnp.where(here, reward[...], 0.0), axis=0, keepdims=True)
        load[pl.ds(j * high + slots * width, AUX), :] = stacked([picked_scale, picked_reward], AUX)


def fetched(table, gathered):
    out = []
    for k in range(table.shape[1]):
        at = table[0, k]
        row = gathered[pl.ds(jnp.maximum(at, 0), 1), :]
        out.append(jnp.where(at >= 0, row, 0.0))
    return out


def back_up(table, gathered, kept, reward, scale, source, out, *refs):
    if len(refs) == 3:
        others, sums, sems = refs
        ends = [pltpu.make_async_copy(source.at[KEPT + i], others.at[i], sems.at[i]) for i in range(others.shape[0])]
        for copy in ends:
            copy.start()
    else:
        others, ends = source, []
        (sums,) = refs
    actions, width, _ = sums.shape
    blocks = [jnp.broadcast_to(b, (8, width)) for b in fetched(table, gathered)]
    weighted = jnp.zeros((actions, width), jnp.float32)
    for start, count, held in ((0, KEPT, kept), (KEPT, actions - KEPT, others)):
        for i in range(count):
            if ends and held is others:
                ends[i].wait()
            for r in range(0, width, 8):
                rows = pl.ds(r, 8)
                total = held[i, 0, rows, :] * blocks[0]
                for k in range(1, len(blocks)):
                    total += held[i, k, rows, :] * blocks[k]
                sums[start + i, rows, :] = total
        weighted += lane_sums(start, [sums[start + i] for i in range(count)])
    backup = jnp.max(reward[...] + scale[...] * weighted, axis=0, keepdims=True)
    out[...] = jnp.broadcast_to(backup, out.shape)


def evaluated(j, table, gathered, load):
    slots, width = table.shape[1], gathered.shape[1]
    first = j * (slots * width + AUX)
    blocks = fetched(table, gathered)
    total = load[pl.ds(first, width), :] * blocks[0]
    for k in range(1, slots):
        total += load[pl.ds(first + k * width, width), :] * blocks[k]
    weighted = lane_sums(0, [total])[0:1]
    aux = load[pl.ds(first + slots * width, AUX), :]
    return aux[1:2] + aux[0:1] * weighted


def first_evaluation(j, table, gathered, before, held, load, out, bounds):
    change = gathered[...] - before[...]
    top = jnp.max(change)
    bottom = jnp.min(change)
    offset = shift * (bottom + top)
    out[...] = jnp.broadcast_to(evaluated(j, table, gathered, load) + discount * offset, out.shape)
    sweep = lax.broadcasted_iota(jnp.int32, bounds.shape, 0)
    side = lax.broadcasted_iota(jnp.int32, bounds.shape, 1)
    bounds[...] = jnp.where(sweep < j, held[...], jnp.where(side == 0, bottom, top))


def next_evaluation(j, table, gathered, load, out):
    out[...] = jnp.broadcast_to(evaluated(j, table, gathered, load), out.shape)


def last_evaluation(j, table, gathered, load, held, out, bounds):
    out[...] = evaluated(j, table, gathered, load)
    bounds[...] = held[...]


SCALARS = pl.BlockSpec(memory_space=pltpu.SMEM)
VECTORS = pl.BlockSpec(memory_space=pltpu.VMEM)
LEFT = pl.BlockSpec(memory_space=pltpu.HBM)


def shaped(*shape):
    return jax.ShapeDtypeStruct(shape, jnp.float32)


def called(body, given, out_shape, name, scratch=(), limit=8, left=0):
    return pl.pallas_call(
        body,
        out_shape=out_shape,
        in_specs=[SCALARS] + [VECTORS] * (len(given) - 1 - left) + [LEFT] * left,
        out_specs=jax.tree.map(lambda _: VECTORS, out_shape),
        scratch_shapes=list(scratch),
        compiler_params=pltpu.CompilerParams(vmem_limit_bytes=limit * MIB),
        name=name,
    )(*given)


def exchange(rows):
    return lax.all_to_all(rows, AXES, 0, 0, tiled=True)


def local(tiles, counts, col_index, reward, policy, start_values):
    actions, _, slots, width, _ = tiles.shape
    devices = lax.axis_size(AXES)
    tiles = tiles.reshape(actions, slots, width, width)
    all_rows = shaped(devices, width)
    square = pltpu.VMEM((actions, width, width), jnp.float32)
    gathered = exchange(jnp.broadcast_to(start_values[None], (devices, width)))
    given = (col_index, policy, reward, tiles)
    table, scale, load, kept = pl.pallas_call(
        prepare,
        out_shape=(
            jax.ShapeDtypeStruct(col_index.shape, jnp.int32),
            shaped(actions, width),
            shaped(SWEEPS * (slots * width + AUX), width),
            shaped(KEPT, *tiles.shape[1:]),
        ),
        in_specs=[SCALARS] + [LEFT] * 4,
        out_specs=(SCALARS, VECTORS, VECTORS, VECTORS),
        scratch_shapes=[
            pltpu.SMEM(col_index.shape, jnp.int32),
            pltpu.VMEM(policy.shape, jnp.int32),
            pltpu.VMEM(reward.shape, jnp.float32),
            pltpu.VMEM((actions - KEPT, *tiles.shape[1:]), jnp.float32),
            square,
            pltpu.VMEM((SWEEPS, width, width), jnp.float32),
            pltpu.SemaphoreType.DMA((len(CHUNKS), 2)),
            pltpu.SemaphoreType.DMA((3,)),
        ],
        compiler_params=pltpu.CompilerParams(vmem_limit_bytes=8 * MIB),
        name="prepare",
            cost_estimate=pl.CostEstimate(flops=4_000_000, bytes_accessed=8_000_000, transcendentals=0),
    )(counts, *(pltpu.with_memory_space_constraint(x, pltpu.HBM) for x in given))
    bounds = jnp.zeros((SWEEPS, 2), jnp.float32)
    for j in range(SWEEPS):
        if j == 0:
            source = pltpu.with_memory_space_constraint(tiles, pltpu.HBM)
            rest = shaped(actions - KEPT, *tiles.shape[1:])
            given = (table, gathered, kept, reward, scale, source)
            scratch = [square, pltpu.SemaphoreType.DMA((actions - KEPT,))]
            backup, others = called(back_up, given, (all_rows, rest), f"back_up_{j}", scratch, left=1)
        else:
            backup = called(back_up, (table, gathered, kept, reward, scale, others), all_rows, f"back_up_{j}", [square])
        before, gathered = gathered, exchange(backup)
        body = functools.partial(first_evaluation, j)
        made = (all_rows, shaped(SWEEPS, 2))
        current, bounds = called(body, (table, gathered, before, bounds, load), made, f"first_evaluation_{j}")
        gathered = exchange(current)
        if j < SWEEPS - 1:
            current = called(functools.partial(next_evaluation, j), (table, gathered, load), all_rows, f"next_evaluation_{j}")
            gathered = exchange(current)
    body = functools.partial(last_evaluation, SWEEPS - 1)
    current, bounds = called(body, (table, gathered, load, bounds), (shaped(1, width), shaped(SWEEPS, 2)), "last_evaluation")
    return current.reshape(width), bounds


def solution(mesh):
    split = Mesh(mesh.devices.reshape(4, 4, 8, 2), AXES)
    placed = (
        P(None, AXES, None, None, None),
        P(AXES),
        P(AXES, None),
        P(None, AXES),
        P(None, AXES),
        P(AXES),
    )
    return jax.shard_map(local, mesh=split, in_specs=placed, out_specs=(P(AXES), P()), check_vma=False)
```

```python
import functools

import jax
import jax.numpy as jnp
from jax import lax
from jax.experimental import pallas as pl
from jax.experimental.pallas import tpu as pltpu
from jax.sharding import Mesh
from jax.sharding import PartitionSpec as P

SWEEPS = 2
AXES = ("x", "y", "z", "c")
discount = 0.9
shift = discount / (1.0 - discount) * 0.5
MIB = 1 << 20
AUX = 8
CHUNKS = ((0, 32), (32, 32), (64, 32), (96, 24), (120, 8))
KEPT = 10
SLOTS = 4


def pieces(values, count):
    out = []
    for left in reversed(range(count)):
        piece = values.astype(jnp.bfloat16)
        out.append(piece)
        if left:
            values = values - piece.astype(jnp.float32)
    return out


def lane_sums(first, row_values):
    at = lax.broadcasted_iota(jnp.int32, (16, 256), 0)
    out = jnp.zeros((16, 128), jnp.float32)
    for i, values in enumerate(row_values):
        row = jnp.where(at == first + i, 1.0, 0.0).astype(jnp.bfloat16)
        both = jnp.concatenate(pieces(values, 2), axis=1)
        out += lax.dot_general(row, both, (((1,), (1,)), ((), ())), preferred_element_type=jnp.float32)
    return out


def stacked(rows, height):
    at = lax.broadcasted_iota(jnp.int32, (height, rows[0].shape[-1]), 0)
    out = jnp.zeros(at.shape, jnp.float32)
    for i, row in enumerate(rows):
        out = jnp.where(at == i, row, out)
    return out


def chunk(g, tiles, kept, others, sems):
    rows = pl.ds(*CHUNKS[g])
    return [
        pltpu.make_async_copy(tiles.at[pl.ds(0, KEPT), :, rows, :], kept.at[:, :, rows, :], sems.at[g, 0]),
        pltpu.make_async_copy(tiles.at[pl.ds(KEPT, others.shape[0]), :, rows, :], others.at[:, :, rows, :], sems.at[g, 1]),
    ]


def prepare(
    counts, columns_in, policy_in, reward_in, tiles,
    named, scale, load, kept,
    col_index, policy, reward, others, sums, columns, sems, small_sems,
):
    actions, slots, width, _ = tiles.shape
    high = slots * width + AUX
    given = ((columns_in, col_index), (policy_in, policy), (reward_in, reward))
    small = [pltpu.make_async_copy(source, target, small_sems.at[i]) for i, (source, target) in enumerate(given)]
    for copy in small:
        copy.start()
    for g in range(len(CHUNKS)):
        for copy in chunk(g, tiles, kept, others, sems):
            copy.start()
    for copy in small:
        copy.wait()
    blocks = [jnp.where(counts[0] > k, col_index[0, k], -1) for k in range(slots)]
    named[...] = stacked([jnp.full((1, width), block.astype(jnp.float32)) for block in blocks], AUX)
    live = [counts[0] > k for k in range(slots)]
    for j in range(SWEEPS):
        columns[j] = jnp.broadcast_to(policy[pl.ds(j, 1), :].astype(jnp.float32), (width, width)).T
    for g in range(len(CHUNKS)):
        for copy in chunk(g, tiles, kept, others, sems):
            copy.wait()
        for r in range(CHUNKS[g][0], sum(CHUNKS[g]), 8):
            rows = pl.ds(r, 8)
            chosen = [columns[j, rows, :] for j in range(SWEEPS)]
            held = [[jnp.zeros((8, width), jnp.float32) for _ in range(slots)] for _ in range(SWEEPS)]
            for a in range(actions):
                total = None
                for k in range(slots):
                    source, place = (kept, a) if a < KEPT else (others, a - KEPT)
                    tile = jnp.where(live[k], source[place, k, rows, :], 0.0)
                    total = tile if total is None else total + tile
                    for j in range(SWEEPS):
                        held[j][k] = jnp.where(chosen[j] == float(a), tile, held[j][k])
                sums[a, rows, :] = total
            for j in range(SWEEPS):
                for k in range(slots):
                    load[pl.ds(j * high + k * width + r, 8), :] = held[j][k]
    inverse = discount / lane_sums(0, [sums[a] for a in range(actions)])
    scale[...] = inverse
    at = lax.broadcasted_iota(jnp.int32, (actions, width), 0)
    for j in range(SWEEPS):
        here = at == policy[pl.ds(j, 1), :]
        picked_scale = jnp.sum(jnp.where(here, inverse, 0.0), axis=0, keepdims=True)
        picked_reward = jnp.sum(jnp.where(here, reward[...], 0.0), axis=0, keepdims=True)
        load[pl.ds(j * high + slots * width, AUX), :] = stacked([picked_scale, picked_reward], AUX)


def fetched(named, gathered):
    states, width = gathered.shape
    wide = jnp.concatenate([named[...]] * 2, axis=0)
    lane = lax.broadcasted_iota(jnp.int32, wide.shape, 1).astype(jnp.float32)
    chosen = [jnp.where(wide == lane + float(h), 1.0, 0.0).astype(jnp.bfloat16) for h in range(0, states, width)]
    chosen = jnp.concatenate(chosen, axis=1)
    rows = jnp.zeros(wide.shape, jnp.float32)
    for piece in pieces(gathered[...], 3):
        rows += jnp.dot(chosen, piece, preferred_element_type=jnp.float32)
    return [rows[k : k + 1] for k in range(SLOTS)]


def back_up(named, gathered, kept, reward, scale, source, out, *refs):
    if len(refs) == 3:
        others, sums, sems = refs
        ends = [pltpu.make_async_copy(source.at[KEPT + i], others.at[i], sems.at[i]) for i in range(others.shape[0])]
        for copy in ends:
            copy.start()
    else:
        others, ends = source, []
        (sums,) = refs
    actions, width, _ = sums.shape
    blocks = [jnp.broadcast_to(b, (8, width)) for b in fetched(named, gathered)]
    weighted = jnp.zeros((actions, width), jnp.float32)
    for start, count, held in ((0, KEPT, kept), (KEPT, actions - KEPT, others)):
        for i in range(count):
            if ends and held is others:
                ends[i].wait()
            for r in range(0, width, 8):
                rows = pl.ds(r, 8)
                total = held[i, 0, rows, :] * blocks[0]
                for k in range(1, len(blocks)):
                    total += held[i, k, rows, :] * blocks[k]
                sums[start + i, rows, :] = total
        weighted += lane_sums(start, [sums[start + i] for i in range(count)])
    backup = jnp.max(reward[...] + scale[...] * weighted, axis=0, keepdims=True)
    out[...] = jnp.broadcast_to(backup, out.shape)


def evaluated(j, named, gathered, load):
    slots, width = SLOTS, gathered.shape[1]
    first = j * (slots * width + AUX)
    blocks = fetched(named, gathered)
    total = load[pl.ds(first, width), :] * blocks[0]
    for k in range(1, slots):
        total += load[pl.ds(first + k * width, width), :] * blocks[k]
    weighted = lane_sums(0, [total])[0:1]
    aux = load[pl.ds(first + slots * width, AUX), :]
    return aux[1:2] + aux[0:1] * weighted


def first_evaluation(j, named, gathered, before, held, load, out, bounds):
    change = gathered[...] - before[...]
    top = jnp.max(change)
    bottom = jnp.min(change)
    offset = shift * (bottom + top)
    out[...] = jnp.broadcast_to(evaluated(j, named, gathered, load) + discount * offset, out.shape)
    sweep = lax.broadcasted_iota(jnp.int32, bounds.shape, 0)
    side = lax.broadcasted_iota(jnp.int32, bounds.shape, 1)
    bounds[...] = jnp.where(sweep < j, held[...], jnp.where(side == 0, bottom, top))


def next_evaluation(j, named, gathered, load, out):
    out[...] = jnp.broadcast_to(evaluated(j, named, gathered, load), out.shape)


def last_evaluation(j, named, gathered, load, held, out, bounds):
    out[...] = evaluated(j, named, gathered, load)
    bounds[...] = held[...]


SCALARS = pl.BlockSpec(memory_space=pltpu.SMEM)
VECTORS = pl.BlockSpec(memory_space=pltpu.VMEM)
LEFT = pl.BlockSpec(memory_space=pltpu.HBM)


def shaped(*shape):
    return jax.ShapeDtypeStruct(shape, jnp.float32)


def called(body, given, out_shape, name, scratch=(), limit=8, left=0):
    return pl.pallas_call(
        body,
        out_shape=out_shape,
        in_specs=[VECTORS] * (len(given) - left) + [LEFT] * left,
        out_specs=jax.tree.map(lambda _: VECTORS, out_shape),
        scratch_shapes=list(scratch),
        compiler_params=pltpu.CompilerParams(vmem_limit_bytes=limit * MIB),
        name=name,
    )(*given)


def exchange(rows):
    return lax.all_to_all(rows, AXES, 0, 0, tiled=True)


def local(tiles, counts, col_index, reward, policy, start_values):
    actions, _, slots, width, _ = tiles.shape
    devices = lax.axis_size(AXES)
    tiles = tiles.reshape(actions, slots, width, width)
    all_rows = shaped(devices, width)
    square = pltpu.VMEM((actions, width, width), jnp.float32)
    gathered = exchange(jnp.broadcast_to(start_values[None], (devices, width)))
    given = (col_index, policy, reward, tiles)
    named, scale, load, kept = pl.pallas_call(
        prepare,
        out_shape=(
            shaped(AUX, width),
            shaped(actions, width),
            shaped(SWEEPS * (slots * width + AUX), width),
            shaped(KEPT, *tiles.shape[1:]),
        ),
        in_specs=[SCALARS] + [LEFT] * 4,
        out_specs=(VECTORS,) * 4,
        scratch_shapes=[
            pltpu.SMEM(col_index.shape, jnp.int32),
            pltpu.VMEM(policy.shape, jnp.int32),
            pltpu.VMEM(reward.shape, jnp.float32),
            pltpu.VMEM((actions - KEPT, *tiles.shape[1:]), jnp.float32),
            square,
            pltpu.VMEM((SWEEPS, width, width), jnp.float32),
            pltpu.SemaphoreType.DMA((len(CHUNKS), 2)),
            pltpu.SemaphoreType.DMA((3,)),
        ],
        compiler_params=pltpu.CompilerParams(vmem_limit_bytes=8 * MIB),
        name="prepare",
            cost_estimate=pl.CostEstimate(flops=4_000_000, bytes_accessed=8_000_000, transcendentals=0),
    )(counts, *(pltpu.with_memory_space_constraint(x, pltpu.HBM) for x in given))
    bounds = jnp.zeros((SWEEPS, 2), jnp.float32)
    for j in range(SWEEPS):
        if j == 0:
            source = pltpu.with_memory_space_constraint(tiles, pltpu.HBM)
            rest = shaped(actions - KEPT, *tiles.shape[1:])
            given = (named, gathered, kept, reward, scale, source)
            scratch = [square, pltpu.SemaphoreType.DMA((actions - KEPT,))]
            backup, others = called(back_up, given, (all_rows, rest), f"back_up_{j}", scratch, left=1)
        else:
            backup = called(back_up, (named, gathered, kept, reward, scale, others), all_rows, f"back_up_{j}", [square])
        before, gathered = gathered, exchange(backup)
        body = functools.partial(first_evaluation, j)
        made = (all_rows, shaped(SWEEPS, 2))
        current, bounds = called(body, (named, gathered, before, bounds, load), made, f"first_evaluation_{j}")
        gathered = exchange(current)
        if j < SWEEPS - 1:
            current = called(functools.partial(next_evaluation, j), (named, gathered, load), all_rows, f"next_evaluation_{j}")
            gathered = exchange(current)
    body = functools.partial(last_evaluation, SWEEPS - 1)
    current, bounds = called(body, (named, gathered, load, bounds), (shaped(1, width), shaped(SWEEPS, 2)), "last_evaluation")
    return current.reshape(width), bounds


def solution(mesh):
    split = Mesh(mesh.devices.reshape(4, 4, 8, 2), AXES)
    placed = (
        P(None, AXES, None, None, None),
        P(AXES),
        P(AXES, None),
        P(None, AXES),
        P(None, AXES),
        P(AXES),
    )
    return jax.shard_map(local, mesh=split, in_specs=placed, out_specs=(P(AXES), P()), check_vma=False)
```

```python
import functools

import jax
import jax.numpy as jnp
from jax import lax
from jax.experimental import pallas as pl
from jax.experimental.pallas import tpu as pltpu
from jax.sharding import Mesh
from jax.sharding import PartitionSpec as P

SWEEPS = 2
AXES = ("x", "y", "z", "c")
ORDER = ("y", "z", "x", "c")
PLANE = ("y", "z")
LINE = ("x", "c")
discount = 0.9
shift = discount / (1.0 - discount) * 0.5
MIB = 1 << 20
AUX = 8
CHUNKS = ((0, 32), (32, 32), (64, 32), (96, 24), (120, 8))
SLOTS = 4


def pieces(values, count):
    out = []
    for left in reversed(range(count)):
        piece = values.astype(jnp.bfloat16)
        out.append(piece)
        if left:
            values = values - piece.astype(jnp.float32)
    return out


def contract(left, right):
    out = jnp.zeros((left.shape[0], right.shape[1]), jnp.float32)
    for piece in pieces(right, 3):
        out += jnp.dot(left, piece, preferred_element_type=jnp.float32)
    return out


def lane_sums(row_values, places=None):
    at = lax.broadcasted_iota(jnp.int32, (16, 256), 0).astype(jnp.float32)
    out = jnp.zeros((16, 128), jnp.float32)
    for i, values in enumerate(row_values):
        place = jnp.concatenate([places[i]] * 2, axis=1) if places else float(i)
        row = jnp.where(at == place, 1.0, 0.0).astype(jnp.bfloat16)
        both = jnp.concatenate(pieces(values, 2), axis=1)
        out += lax.dot_general(row, both, (((1,), (1,)), ((), ())), preferred_element_type=jnp.float32)
    return out


def stacked(rows, height, places=None):
    at = lax.broadcasted_iota(jnp.int32, (height, rows[0].shape[-1]), 0).astype(jnp.float32)
    out = jnp.zeros(at.shape, jnp.float32)
    for i, row in enumerate(rows):
        out = jnp.where(at == (places[i] if places else float(i)), row, out)
    return out


def chunk(g, tiles, kept, sems):
    rows = pl.ds(*CHUNKS[g])
    return pltpu.make_async_copy(tiles.at[:, :, rows, :], kept.at[:, :, rows, :], sems.at[g])


def prepare(
    counts, at, columns_in, policy_in, reward_in, tiles,
    named, scale, load, kept,
    col_index, policy, reward, sums, columns, sems, small_sems,
):
    actions, slots, width, _ = tiles.shape
    high = slots * width + AUX
    given = ((columns_in, col_index), (policy_in, policy), (reward_in, reward))
    small = [pltpu.make_async_copy(source, target, small_sems.at[i]) for i, (source, target) in enumerate(given)]
    for copy in small:
        copy.start()
    for g in range(len(CHUNKS)):
        chunk(g, tiles, kept, sems).start()
    for copy in small:
        copy.wait()
    columns_of = []
    for k in range(slots):
        block = col_index[0, k]
        place = (block % 64) // 2 * 8 + block // 64 * 2 + block % 2
        place = jnp.where(counts[0] > k, place, -1)
        columns_of.append(jnp.full((1, width), place.astype(jnp.float32)))
    named[...] = stacked(columns_of, AUX)
    columns_of.append(jnp.full((1, width), at[0, 0].astype(jnp.float32)))
    live = [counts[0] > k for k in range(slots)]
    for j in range(SWEEPS):
        columns[j] = jnp.broadcast_to(policy[pl.ds(j, 1), :].astype(jnp.float32), (width, width)).T
    for g in range(len(CHUNKS)):
        chunk(g, tiles, kept, sems).wait()
        for r in range(CHUNKS[g][0], sum(CHUNKS[g]), 8):
            rows = pl.ds(r, 8)
            chosen = [columns[j, rows, :] for j in range(SWEEPS)]
            held = [[jnp.zeros((8, width), jnp.float32) for _ in range(slots)] for _ in range(SWEEPS)]
            for a in range(actions):
                total = None
                for k in range(slots):
                    tile = jnp.where(live[k], kept[a, k, rows, :], 0.0)
                    total = tile if total is None else total + tile
                    for j in range(SWEEPS):
                        held[j][k] = jnp.where(chosen[j] == float(a), tile, held[j][k])
                sums[a, rows, :] = total
            for j in range(SWEEPS):
                for k in range(slots):
                    load[pl.ds(j * high + k * width + r, 8), :] = held[j][k]
    inverse = discount / lane_sums([sums[a] for a in range(actions)])
    scale[...] = inverse
    action = lax.broadcasted_iota(jnp.int32, (actions, width), 0)
    for j in range(SWEEPS):
        here = action == policy[pl.ds(j, 1), :]
        picked_scale = jnp.sum(jnp.where(here, inverse, 0.0), axis=0, keepdims=True)
        picked_reward = jnp.sum(jnp.where(here, reward[...], 0.0), axis=0, keepdims=True)
        load[pl.ds(j * high + slots * width, AUX), :] = stacked([picked_scale, picked_reward] + columns_of, AUX)


def fetched(named, gathered):
    states, width = gathered.shape
    lane = lax.broadcasted_iota(jnp.int32, named.shape, 1).astype(jnp.float32)
    chosen = [jnp.where(named == lane + float(h), 1.0, 0.0).astype(jnp.bfloat16) for h in range(0, states, width)]
    return contract(jnp.concatenate(chosen, axis=1), gathered[...])


def back_up(named, gathered, tiles, reward, scale, out, sums):
    actions, width, _ = sums.shape
    rows_of = fetched(jnp.concatenate([named[...]] * 2, axis=0), gathered)
    blocks = [jnp.broadcast_to(rows_of[k : k + 1], (8, width)) for k in range(SLOTS)]
    for a in range(actions):
        for r in range(0, width, 8):
            rows = pl.ds(r, 8)
            total = tiles[a, 0, rows, :] * blocks[0]
            for k in range(1, SLOTS):
                total += tiles[a, k, rows, :] * blocks[k]
            sums[a, rows, :] = total
    weighted = lane_sums([sums[a] for a in range(actions)])
    backup = jnp.max(reward[...] + scale[...] * weighted, axis=0, keepdims=True)
    out[...] = jnp.broadcast_to(backup, out.shape)


def products(load, first, rows_of, start):
    width = load.shape[1]
    total = load[pl.ds(first, width), :] * rows_of[start : start + 1]
    for k in range(1, SLOTS):
        total += load[pl.ds(first + k * width, width), :] * rows_of[start + k : start + k + 1]
    return total


def line_product(j, gathered, loads):
    width = gathered.shape[1]
    first = j * (SLOTS * width + AUX)
    aux = [load[pl.ds(first + SLOTS * width, AUX), :] for load in loads]
    rows_of = fetched(jnp.concatenate(aux, axis=0), gathered)
    owners = [a[2 + SLOTS : 3 + SLOTS] for a in aux]
    weighted = lane_sums([products(load, first, rows_of, b * AUX + 2) for b, load in enumerate(loads)], owners)[:8]
    return stacked([a[1:2] for a in aux], 8, owners) + stacked([a[0:1] for a in aux], 8, owners) * weighted


def spread_out(out, got):
    for i in range(out.shape[0] // 8):
        out[pl.ds(i * 8, 8), :] = got


def first_evaluation(j, gathered, before, held, *refs):
    *loads, out, bounds = refs
    change = gathered[...] - before[...]
    top = jnp.max(change)
    bottom = jnp.min(change)
    offset = shift * (bottom + top)
    spread_out(out, line_product(j, gathered, loads) + discount * offset)
    sweep = lax.broadcasted_iota(jnp.int32, bounds.shape, 0)
    side = lax.broadcasted_iota(jnp.int32, bounds.shape, 1)
    bounds[...] = jnp.where(sweep < j, held[...], jnp.where(side == 0, bottom, top))


def next_evaluation(j, gathered, *refs):
    *loads, out = refs
    spread_out(out, line_product(j, gathered, loads))


def last_evaluation(j, named, gathered, load, held, out, bounds):
    width = gathered.shape[1]
    first = j * (SLOTS * width + AUX)
    rows_of = fetched(jnp.concatenate([named[...]] * 2, axis=0), gathered)
    weighted = lane_sums([products(load, first, rows_of, 0)])[0:1]
    aux = load[pl.ds(first + SLOTS * width, AUX), :]
    out[...] = aux[1:2] + aux[0:1] * weighted
    bounds[...] = held[...]


SCALARS = pl.BlockSpec(memory_space=pltpu.SMEM)
VECTORS = pl.BlockSpec(memory_space=pltpu.VMEM)
LEFT = pl.BlockSpec(memory_space=pltpu.HBM)


def shaped(*shape):
    return jax.ShapeDtypeStruct(shape, jnp.float32)


def called(body, given, out_shape, name, scratch=(), limit=8, left=0):
    return pl.pallas_call(
        body,
        out_shape=out_shape,
        in_specs=[VECTORS] * (len(given) - left) + [LEFT] * left,
        out_specs=jax.tree.map(lambda _: VECTORS, out_shape),
        scratch_shapes=list(scratch),
        compiler_params=pltpu.CompilerParams(vmem_limit_bytes=limit * MIB),
        name=name,
    )(*given)


def over_all(rows):
    return lax.all_to_all(rows, ORDER, 0, 0, tiled=True)


def over_plane(rows):
    return lax.all_to_all(rows, PLANE, 0, 0, tiled=True)


def local(tiles, counts, col_index, reward, policy, start_values):
    actions, _, slots, width, _ = tiles.shape
    devices = lax.axis_size(AXES)
    tiles = tiles.reshape(actions, slots, width, width)
    all_rows = shaped(devices, width)
    square = pltpu.VMEM((actions, width, width), jnp.float32)
    gathered = over_all(jnp.broadcast_to(start_values[None], (devices, width)))
    given = (col_index, policy, reward, tiles)
    named, scale, load, kept = pl.pallas_call(
        prepare,
        out_shape=(
            shaped(AUX, width),
            shaped(actions, width),
            shaped(SWEEPS * (slots * width + AUX), width),
            shaped(*tiles.shape),
        ),
        in_specs=[SCALARS] * 2 + [LEFT] * 4,
        out_specs=(VECTORS,) * 4,
        scratch_shapes=[
            pltpu.SMEM(col_index.shape, jnp.int32),
            pltpu.VMEM(policy.shape, jnp.int32),
            pltpu.VMEM(reward.shape, jnp.float32),
            square,
            pltpu.VMEM((SWEEPS, width, width), jnp.float32),
            pltpu.SemaphoreType.DMA((len(CHUNKS),)),
            pltpu.SemaphoreType.DMA((3,)),
        ],
        compiler_params=pltpu.CompilerParams(vmem_limit_bytes=8 * MIB),
        name="prepare",
            cost_estimate=pl.CostEstimate(flops=4_000_000, bytes_accessed=8_000_000, transcendentals=0),
    )(counts, lax.axis_index(LINE).reshape(1, 1), *(pltpu.with_memory_space_constraint(x, pltpu.HBM) for x in given))
    far = lax.axis_size(LINE[0])
    loads = [load] + [lax.ppermute(load, LINE[0], [(i, (i + k) % far) for i in range(far)]) for k in range(1, far)]
    bounds = jnp.zeros((SWEEPS, 2), jnp.float32)
    all_rows = shaped(devices, width)
    for j in range(SWEEPS):
        backup = called(back_up, (named, gathered, kept, reward, scale), all_rows, f"back_up_{j}", [square])
        before, gathered = gathered, over_all(backup)
        if j == 0:
            *loads, gathered = lax.optimization_barrier((*loads, gathered))
            loads += [lax.ppermute(held, LINE[1], [(0, 1), (1, 0)]) for held in loads]
        body = functools.partial(first_evaluation, j)
        made = (all_rows, shaped(SWEEPS, 2))
        current, bounds = called(body, (gathered, before, bounds, *loads), made, f"first_evaluation_{j}")
        gathered = over_plane(current)
        if j < SWEEPS - 1:
            current = called(functools.partial(next_evaluation, j), (gathered, *loads), all_rows, f"next_evaluation_{j}")
            gathered = over_plane(current)
    body = functools.partial(last_evaluation, SWEEPS - 1)
    current, bounds = called(body, (named, gathered, load, bounds), (shaped(1, width), shaped(SWEEPS, 2)), "last_evaluation")
    return current.reshape(width), bounds


def solution(mesh):
    split = Mesh(mesh.devices.reshape(4, 4, 8, 2), AXES)
    placed = (
        P(None, AXES, None, None, None),
        P(AXES),
        P(AXES, None),
        P(None, AXES),
        P(None, AXES),
        P(AXES),
    )
    return jax.shard_map(local, mesh=split, in_specs=placed, out_specs=(P(AXES), P()), check_vma=False)
```

```python
import functools

import jax
import jax.numpy as jnp
from jax import lax
from jax.experimental import pallas as pl
from jax.experimental.pallas import tpu as pltpu
from jax.sharding import Mesh
from jax.sharding import PartitionSpec as P

SWEEPS = 2
AXES = ("x", "y", "z", "c")
ORDER = ("y", "z", "x", "c")
PLANE = ("y", "z")
LINE = ("x", "c")
discount = 0.9
shift = discount / (1.0 - discount) * 0.5
MIB = 1 << 20
AUX = 8
CHUNKS = ((0, 32), (32, 32), (64, 32), (96, 24), (120, 8))
SLOTS = 4


def pieces(values, count):
    out = []
    for left in reversed(range(count)):
        piece = values.astype(jnp.bfloat16)
        out.append(piece)
        if left:
            values = values - piece.astype(jnp.float32)
    return out


def contract(left, right):
    out = jnp.zeros((left.shape[0], right.shape[1]), jnp.float32)
    for piece in pieces(right, 3):
        out += jnp.dot(left, piece, preferred_element_type=jnp.float32)
    return out


def lane_sums(row_values, places=None):
    at = lax.broadcasted_iota(jnp.int32, (16, 256), 0).astype(jnp.float32)
    out = jnp.zeros((16, 128), jnp.float32)
    for i, values in enumerate(row_values):
        place = jnp.concatenate([places[i]] * 2, axis=1) if places else float(i)
        row = jnp.where(at == place, 1.0, 0.0).astype(jnp.bfloat16)
        both = jnp.concatenate(pieces(values, 2), axis=1)
        out += lax.dot_general(row, both, (((1,), (1,)), ((), ())), preferred_element_type=jnp.float32)
    return out


def stacked(rows, height, places=None):
    at = lax.broadcasted_iota(jnp.int32, (height, rows[0].shape[-1]), 0).astype(jnp.float32)
    out = jnp.zeros(at.shape, jnp.float32)
    for i, row in enumerate(rows):
        out = jnp.where(at == (places[i] if places else float(i)), row, out)
    return out


def chunk(g, tiles, kept, sems):
    rows = pl.ds(*CHUNKS[g])
    return pltpu.make_async_copy(tiles.at[:, :, rows, :], kept.at[:, :, rows, :], sems.at[g])


def prepare(
    counts, at, columns_in, policy_in, reward_in, tiles,
    named, scale, load, kept,
    col_index, policy, reward, sums, columns, sems, small_sems,
):
    actions, slots, width, _ = tiles.shape
    high = slots * width + AUX
    given = ((columns_in, col_index), (policy_in, policy), (reward_in, reward))
    small = [pltpu.make_async_copy(source, target, small_sems.at[i]) for i, (source, target) in enumerate(given)]
    for copy in small:
        copy.start()
    for g in range(len(CHUNKS)):
        chunk(g, tiles, kept, sems).start()
    for copy in small:
        copy.wait()
    columns_of = []
    for k in range(slots):
        block = col_index[0, k]
        place = (block % 64) // 2 * 8 + block // 64 * 2 + block % 2
        place = jnp.where(counts[0] > k, place, -1)
        columns_of.append(jnp.full((1, width), place.astype(jnp.float32)))
    named[...] = stacked(columns_of, AUX)
    columns_of.append(jnp.full((1, width), at[0, 0].astype(jnp.float32)))
    live = [counts[0] > k for k in range(slots)]
    for j in range(SWEEPS):
        columns[j] = jnp.broadcast_to(policy[pl.ds(j, 1), :].astype(jnp.float32), (width, width)).T
    for g in range(len(CHUNKS)):
        chunk(g, tiles, kept, sems).wait()
        for r in range(CHUNKS[g][0], sum(CHUNKS[g]), 8):
            rows = pl.ds(r, 8)
            chosen = [columns[j, rows, :] for j in range(SWEEPS)]
            held = [[jnp.zeros((8, width), jnp.float32) for _ in range(slots)] for _ in range(SWEEPS)]
            for a in range(actions):
                total = None
                for k in range(slots):
                    tile = jnp.where(live[k], kept[a, k, rows, :], 0.0)
                    total = tile if total is None else total + tile
                    for j in range(SWEEPS):
                        held[j][k] = jnp.where(chosen[j] == float(a), tile, held[j][k])
                sums[a, rows, :] = total
            for j in range(SWEEPS):
                for k in range(slots):
                    load[pl.ds(j * high + k * width + r, 8), :] = held[j][k]
    inverse = discount / lane_sums([sums[a] for a in range(actions)])
    scale[...] = inverse
    action = lax.broadcasted_iota(jnp.int32, (actions, width), 0)
    for j in range(SWEEPS):
        here = action == policy[pl.ds(j, 1), :]
        picked_scale = jnp.sum(jnp.where(here, inverse, 0.0), axis=0, keepdims=True)
        picked_reward = jnp.sum(jnp.where(here, reward[...], 0.0), axis=0, keepdims=True)
        load[pl.ds(j * high + slots * width, AUX), :] = stacked([picked_scale, picked_reward] + columns_of, AUX)


def fetched(named, gathered):
    states, width = gathered.shape
    lane = lax.broadcasted_iota(jnp.int32, named.shape, 1).astype(jnp.float32)
    chosen = [jnp.where(named == lane + float(h), 1.0, 0.0).astype(jnp.bfloat16) for h in range(0, states, width)]
    return contract(jnp.concatenate(chosen, axis=1), gathered[...])


def back_up(named, gathered, tiles, reward, scale, out, sums):
    actions, width, _ = sums.shape
    rows_of = fetched(jnp.concatenate([named[...]] * 2, axis=0), gathered)
    blocks = [jnp.broadcast_to(rows_of[k : k + 1], (8, width)) for k in range(SLOTS)]
    for a in range(actions):
        for r in range(0, width, 8):
            rows = pl.ds(r, 8)
            total = tiles[a, 0, rows, :] * blocks[0]
            for k in range(1, SLOTS):
                total += tiles[a, k, rows, :] * blocks[k]
            sums[a, rows, :] = total
    weighted = lane_sums([sums[a] for a in range(actions)])
    backup = jnp.max(reward[...] + scale[...] * weighted, axis=0, keepdims=True)
    out[...] = jnp.broadcast_to(backup, out.shape)


def products(load, first, rows_of, start):
    width = load.shape[1]
    total = load[pl.ds(first, width), :] * rows_of[start : start + 1]
    for k in range(1, SLOTS):
        total += load[pl.ds(first + k * width, width), :] * rows_of[start + k : start + k + 1]
    return total


def line_product(j, gathered, loads):
    width = gathered.shape[1]
    first = j * (SLOTS * width + AUX)
    aux = [load[pl.ds(first + SLOTS * width, AUX), :] for load in loads]
    rows_of = fetched(jnp.concatenate(aux, axis=0), gathered)
    owners = [a[2 + SLOTS : 3 + SLOTS] for a in aux]
    weighted = lane_sums([products(load, first, rows_of, b * AUX + 2) for b, load in enumerate(loads)], owners)[:8]
    return stacked([a[1:2] for a in aux], 8, owners) + stacked([a[0:1] for a in aux], 8, owners) * weighted


def spread_out(out, got):
    for i in range(out.shape[0] // 8):
        out[pl.ds(i * 8, 8), :] = got


def first_evaluation(j, gathered, before, held, *refs):
    *loads, out, bounds = refs
    change = gathered[...] - before[...]
    top = jnp.max(change)
    bottom = jnp.min(change)
    offset = shift * (bottom + top)
    spread_out(out, line_product(j, gathered, loads) + discount * offset)
    sweep = lax.broadcasted_iota(jnp.int32, bounds.shape, 0)
    side = lax.broadcasted_iota(jnp.int32, bounds.shape, 1)
    bounds[...] = jnp.where(sweep < j, held[...], jnp.where(side == 0, bottom, top))


def next_evaluation(j, gathered, *refs):
    *loads, out = refs
    spread_out(out, line_product(j, gathered, loads))


def last_evaluation(j, named, gathered, load, held, out, bounds):
    width = gathered.shape[1]
    first = j * (SLOTS * width + AUX)
    rows_of = fetched(jnp.concatenate([named[...]] * 2, axis=0), gathered)
    weighted = lane_sums([products(load, first, rows_of, 0)])[0:1]
    aux = load[pl.ds(first + SLOTS * width, AUX), :]
    out[...] = aux[1:2] + aux[0:1] * weighted
    bounds[...] = held[...]


SCALARS = pl.BlockSpec(memory_space=pltpu.SMEM)
VECTORS = pl.BlockSpec(memory_space=pltpu.VMEM)
LEFT = pl.BlockSpec(memory_space=pltpu.HBM)


def shaped(*shape):
    return jax.ShapeDtypeStruct(shape, jnp.float32)


def called(body, given, out_shape, name, scratch=(), limit=8, left=0):
    return pl.pallas_call(
        body,
        out_shape=out_shape,
        in_specs=[VECTORS] * (len(given) - left) + [LEFT] * left,
        out_specs=jax.tree.map(lambda _: VECTORS, out_shape),
        scratch_shapes=list(scratch),
        compiler_params=pltpu.CompilerParams(vmem_limit_bytes=limit * MIB),
        name=name,
    )(*given)


def over_all(rows):
    return lax.all_to_all(rows, ORDER, 0, 0, tiled=True)


def over_plane(rows):
    return lax.all_to_all(rows, PLANE, 0, 0, tiled=True)


def local(tiles, counts, col_index, reward, policy, start_values):
    actions, _, slots, width, _ = tiles.shape
    devices = lax.axis_size(AXES)
    tiles = tiles.reshape(actions, slots, width, width)
    all_rows = shaped(devices, width)
    square = pltpu.VMEM((actions, width, width), jnp.float32)
    gathered = over_all(jnp.broadcast_to(start_values[None], (devices, width)))
    given = (col_index, policy, reward, tiles)
    named, scale, load, kept = pl.pallas_call(
        prepare,
        out_shape=(
            shaped(AUX, width),
            shaped(actions, width),
            shaped(SWEEPS * (slots * width + AUX), width),
            shaped(*tiles.shape),
        ),
        in_specs=[SCALARS] * 2 + [LEFT] * 4,
        out_specs=(VECTORS,) * 4,
        scratch_shapes=[
            pltpu.SMEM(col_index.shape, jnp.int32),
            pltpu.VMEM(policy.shape, jnp.int32),
            pltpu.VMEM(reward.shape, jnp.float32),
            square,
            pltpu.VMEM((SWEEPS, width, width), jnp.float32),
            pltpu.SemaphoreType.DMA((len(CHUNKS),)),
            pltpu.SemaphoreType.DMA((3,)),
        ],
        compiler_params=pltpu.CompilerParams(vmem_limit_bytes=8 * MIB),
        name="prepare",
            cost_estimate=pl.CostEstimate(flops=4_000_000, bytes_accessed=8_000_000, transcendentals=0),
    )(counts, lax.axis_index(LINE).reshape(1, 1), *(pltpu.with_memory_space_constraint(x, pltpu.HBM) for x in given))
    far = lax.axis_size(LINE[0])
    loads = [load] + [lax.ppermute(load, LINE[0], [(i, (i + k) % far) for i in range(far)]) for k in range(1, far)]
    near = lax.ppermute(load, LINE[1], [(0, 1), (1, 0)])
    *others, gathered = lax.optimization_barrier((*loads[1:], gathered))
    loads = [load, *others, near] + [lax.ppermute(held, LINE[1], [(0, 1), (1, 0)]) for held in others]
    bounds = jnp.zeros((SWEEPS, 2), jnp.float32)
    all_rows = shaped(devices, width)
    for j in range(SWEEPS):
        backup = called(back_up, (named, gathered, kept, reward, scale), all_rows, f"back_up_{j}", [square])
        before, gathered = gathered, over_all(backup)
        body = functools.partial(first_evaluation, j)
        made = (all_rows, shaped(SWEEPS, 2))
        current, bounds = called(body, (gathered, before, bounds, *loads), made, f"first_evaluation_{j}")
        gathered = over_plane(current)
        if j < SWEEPS - 1:
            current = called(functools.partial(next_evaluation, j), (gathered, *loads), all_rows, f"next_evaluation_{j}")
            gathered = over_plane(current)
    body = functools.partial(last_evaluation, SWEEPS - 1)
    current, bounds = called(body, (named, gathered, load, bounds), (shaped(1, width), shaped(SWEEPS, 2)), "last_evaluation")
    return current.reshape(width), bounds


def solution(mesh):
    split = Mesh(mesh.devices.reshape(4, 4, 8, 2), AXES)
    placed = (
        P(None, AXES, None, None, None),
        P(AXES),
        P(AXES, None),
        P(None, AXES),
        P(None, AXES),
        P(AXES),
    )
    return jax.shard_map(local, mesh=split, in_specs=placed, out_specs=(P(AXES), P()), check_vma=False)
```

```python
import functools

import jax
import jax.numpy as jnp
from jax import lax
from jax.experimental import pallas as pl
from jax.experimental.pallas import tpu as pltpu
from jax.sharding import Mesh
from jax.sharding import PartitionSpec as P

SWEEPS = 2
AXES = ("x", "y", "z", "c")
ORDER = ("y", "z", "x", "c")
PLANE = ("y", "z")
LINE = ("x", "c")
discount = 0.9
shift = discount / (1.0 - discount) * 0.5
MIB = 1 << 20
AUX = 8
CHUNKS = ((0, 32), (32, 32), (64, 32), (96, 24), (120, 8))
SLOTS = 4


def pieces(values, count):
    out = []
    for left in reversed(range(count)):
        piece = values.astype(jnp.bfloat16)
        out.append(piece)
        if left:
            values = values - piece.astype(jnp.float32)
    return out


def contract(left, right):
    out = jnp.zeros((left.shape[0], right.shape[1]), jnp.float32)
    for piece in pieces(right, 3):
        out += jnp.dot(left, piece, preferred_element_type=jnp.float32)
    return out


def lane_sums(row_values, places=None):
    at = lax.broadcasted_iota(jnp.int32, (16, 256), 0).astype(jnp.float32)
    out = jnp.zeros((16, 128), jnp.float32)
    for i, values in enumerate(row_values):
        place = jnp.concatenate([places[i]] * 2, axis=1) if places else float(i)
        row = jnp.where(at == place, 1.0, 0.0).astype(jnp.bfloat16)
        both = jnp.concatenate(pieces(values, 2), axis=1)
        out += lax.dot_general(row, both, (((1,), (1,)), ((), ())), preferred_element_type=jnp.float32)
    return out


def stacked(rows, height, places=None):
    at = lax.broadcasted_iota(jnp.int32, (height, rows[0].shape[-1]), 0).astype(jnp.float32)
    out = jnp.zeros(at.shape, jnp.float32)
    for i, row in enumerate(rows):
        out = jnp.where(at == (places[i] if places else float(i)), row, out)
    return out


def chunk(g, tiles, kept, sems):
    rows = pl.ds(*CHUNKS[g])
    return pltpu.make_async_copy(tiles.at[:, :, rows, :], kept.at[:, :, rows, :], sems.at[g])


def prepare(
    counts, at, columns_in, policy_in, reward_in, tiles,
    named, scale, load, kept,
    col_index, policy, reward, sums, columns, sems, small_sems,
):
    actions, slots, width, _ = tiles.shape
    high = slots * width + AUX
    given = ((columns_in, col_index), (policy_in, policy), (reward_in, reward))
    small = [pltpu.make_async_copy(source, target, small_sems.at[i]) for i, (source, target) in enumerate(given)]
    for copy in small:
        copy.start()
    for g in range(len(CHUNKS)):
        chunk(g, tiles, kept, sems).start()
    for copy in small:
        copy.wait()
    columns_of = []
    for k in range(slots):
        block = col_index[0, k]
        place = (block % 64) // 2 * 8 + block // 64 * 2 + block % 2
        place = jnp.where(counts[0] > k, place, -1)
        columns_of.append(jnp.full((1, width), place.astype(jnp.float32)))
    named[...] = stacked(columns_of, AUX)
    columns_of.append(jnp.full((1, width), at[0, 0].astype(jnp.float32)))
    live = [counts[0] > k for k in range(slots)]
    for j in range(SWEEPS):
        columns[j] = jnp.broadcast_to(policy[pl.ds(j, 1), :].astype(jnp.float32), (width, width)).T
    for g in range(len(CHUNKS)):
        chunk(g, tiles, kept, sems).wait()
        for r in range(CHUNKS[g][0], sum(CHUNKS[g]), 8):
            rows = pl.ds(r, 8)
            chosen = [columns[j, rows, :] for j in range(SWEEPS)]
            held = [[jnp.zeros((8, width), jnp.float32) for _ in range(slots)] for _ in range(SWEEPS)]
            for a in range(actions):
                total = None
                for k in range(slots):
                    tile = jnp.where(live[k], kept[a, k, rows, :], 0.0)
                    total = tile if total is None else total + tile
                    for j in range(SWEEPS):
                        held[j][k] = jnp.where(chosen[j] == float(a), tile, held[j][k])
                sums[a, rows, :] = total
            for j in range(SWEEPS):
                for k in range(slots):
                    load[pl.ds(j * high + k * width + r, 8), :] = held[j][k]
    inverse = discount / lane_sums([sums[a] for a in range(actions)])
    scale[...] = inverse
    action = lax.broadcasted_iota(jnp.int32, (actions, width), 0)
    for j in range(SWEEPS):
        here = action == policy[pl.ds(j, 1), :]
        picked_scale = jnp.sum(jnp.where(here, inverse, 0.0), axis=0, keepdims=True)
        picked_reward = jnp.sum(jnp.where(here, reward[...], 0.0), axis=0, keepdims=True)
        load[pl.ds(j * high + slots * width, AUX), :] = stacked([picked_scale, picked_reward] + columns_of, AUX)


def fetched(named, gathered):
    states, width = gathered.shape
    lane = lax.broadcasted_iota(jnp.int32, named.shape, 1).astype(jnp.float32)
    chosen = [jnp.where(named == lane + float(h), 1.0, 0.0).astype(jnp.bfloat16) for h in range(0, states, width)]
    return contract(jnp.concatenate(chosen, axis=1), gathered[...])


def back_up(named, gathered, tiles, reward, scale, out, sums):
    actions, width, _ = sums.shape
    rows_of = fetched(jnp.concatenate([named[...]] * 2, axis=0), gathered)
    blocks = [jnp.broadcast_to(rows_of[k : k + 1], (8, width)) for k in range(SLOTS)]
    for a in range(actions):
        for r in range(0, width, 8):
            rows = pl.ds(r, 8)
            total = tiles[a, 0, rows, :] * blocks[0]
            for k in range(1, SLOTS):
                total += tiles[a, k, rows, :] * blocks[k]
            sums[a, rows, :] = total
    weighted = lane_sums([sums[a] for a in range(actions)])
    backup = jnp.max(reward[...] + scale[...] * weighted, axis=0, keepdims=True)
    out[...] = jnp.broadcast_to(backup, out.shape)


def products(load, first, rows_of, start):
    width = load.shape[1]
    total = load[pl.ds(first, width), :] * rows_of[start : start + 1]
    for k in range(1, SLOTS):
        total += load[pl.ds(first + k * width, width), :] * rows_of[start + k : start + k + 1]
    return total


def line_product(j, gathered, loads):
    width = gathered.shape[1]
    first = j * (SLOTS * width + AUX)
    aux = [load[pl.ds(first + SLOTS * width, AUX), :] for load in loads]
    rows_of = fetched(jnp.concatenate(aux, axis=0), gathered)
    owners = [a[2 + SLOTS : 3 + SLOTS] for a in aux]
    weighted = lane_sums([products(load, first, rows_of, b * AUX + 2) for b, load in enumerate(loads)], owners)[:8]
    return stacked([a[1:2] for a in aux], 8, owners) + stacked([a[0:1] for a in aux], 8, owners) * weighted


def spread_out(out, got):
    for i in range(out.shape[0] // 8):
        out[pl.ds(i * 8, 8), :] = got


def first_evaluation(j, gathered, before, held, *refs):
    *loads, out, bounds = refs
    change = gathered[...] - before[...]
    top = jnp.max(change)
    bottom = jnp.min(change)
    offset = shift * (bottom + top)
    spread_out(out, line_product(j, gathered, loads) + discount * offset)
    sweep = lax.broadcasted_iota(jnp.int32, bounds.shape, 0)
    side = lax.broadcasted_iota(jnp.int32, bounds.shape, 1)
    bounds[...] = jnp.where(sweep < j, held[...], jnp.where(side == 0, bottom, top))


def next_evaluation(j, gathered, *refs):
    *loads, out = refs
    spread_out(out, line_product(j, gathered, loads))


def last_evaluation(j, named, gathered, load, held, out, bounds):
    width = gathered.shape[1]
    first = j * (SLOTS * width + AUX)
    rows_of = fetched(jnp.concatenate([named[...]] * 2, axis=0), gathered)
    weighted = lane_sums([products(load, first, rows_of, 0)])[0:1]
    aux = load[pl.ds(first + SLOTS * width, AUX), :]
    out[...] = aux[1:2] + aux[0:1] * weighted
    bounds[...] = held[...]


SCALARS = pl.BlockSpec(memory_space=pltpu.SMEM)
VECTORS = pl.BlockSpec(memory_space=pltpu.VMEM)
LEFT = pl.BlockSpec(memory_space=pltpu.HBM)


def shaped(*shape):
    return jax.ShapeDtypeStruct(shape, jnp.float32)


def called(body, given, out_shape, name, scratch=(), limit=8, left=0):
    return pl.pallas_call(
        body,
        out_shape=out_shape,
        in_specs=[VECTORS] * (len(given) - left) + [LEFT] * left,
        out_specs=jax.tree.map(lambda _: VECTORS, out_shape),
        scratch_shapes=list(scratch),
        compiler_params=pltpu.CompilerParams(vmem_limit_bytes=limit * MIB),
        name=name,
    )(*given)


def over_all(rows):
    return lax.all_to_all(rows, ORDER, 0, 0, tiled=True)


def over_plane(rows):
    return lax.all_to_all(rows, PLANE, 0, 0, tiled=True)


def local(tiles, counts, col_index, reward, policy, start_values):
    actions, _, slots, width, _ = tiles.shape
    devices = lax.axis_size(AXES)
    tiles = tiles.reshape(actions, slots, width, width)
    all_rows = shaped(devices, width)
    square = pltpu.VMEM((actions, width, width), jnp.float32)
    gathered = over_all(jnp.broadcast_to(start_values[None], (devices, width)))
    given = (col_index, policy, reward, tiles)
    named, scale, load, kept = pl.pallas_call(
        prepare,
        out_shape=(
            shaped(AUX, width),
            shaped(actions, width),
            shaped(SWEEPS * (slots * width + AUX), width),
            shaped(*tiles.shape),
        ),
        in_specs=[SCALARS] * 2 + [LEFT] * 4,
        out_specs=(VECTORS,) * 4,
        scratch_shapes=[
            pltpu.SMEM(col_index.shape, jnp.int32),
            pltpu.VMEM(policy.shape, jnp.int32),
            pltpu.VMEM(reward.shape, jnp.float32),
            square,
            pltpu.VMEM((SWEEPS, width, width), jnp.float32),
            pltpu.SemaphoreType.DMA((len(CHUNKS),)),
            pltpu.SemaphoreType.DMA((3,)),
        ],
        compiler_params=pltpu.CompilerParams(vmem_limit_bytes=8 * MIB),
        name="prepare",
            cost_estimate=pl.CostEstimate(flops=4_000_000, bytes_accessed=8_000_000, transcendentals=0),
    )(counts, lax.axis_index(LINE).reshape(1, 1), *(pltpu.with_memory_space_constraint(x, pltpu.HBM) for x in given))
    far = lax.axis_size(LINE[0])
    loads = [load] + [lax.ppermute(load, LINE[0], [(i, (i + k) % far) for i in range(far)]) for k in range(1, far)]
    *loads, gathered = lax.optimization_barrier((*loads, gathered))
    loads += [lax.ppermute(held, LINE[1], [(0, 1), (1, 0)]) for held in loads]
    bounds = jnp.zeros((SWEEPS, 2), jnp.float32)
    all_rows = shaped(devices, width)
    for j in range(SWEEPS):
        backup = called(back_up, (named, gathered, kept, reward, scale), all_rows, f"back_up_{j}", [square])
        before, gathered = gathered, over_all(backup)
        body = functools.partial(first_evaluation, j)
        made = (all_rows, shaped(SWEEPS, 2))
        current, bounds = called(body, (gathered, before, bounds, *loads), made, f"first_evaluation_{j}")
        gathered = over_plane(current)
        if j < SWEEPS - 1:
            current = called(functools.partial(next_evaluation, j), (gathered, *loads), all_rows, f"next_evaluation_{j}")
            gathered = over_plane(current)
    body = functools.partial(last_evaluation, SWEEPS - 1)
    current, bounds = called(body, (named, gathered, load, bounds), (shaped(1, width), shaped(SWEEPS, 2)), "last_evaluation")
    return current.reshape(width), bounds


def solution(mesh):
    split = Mesh(mesh.devices.reshape(4, 4, 8, 2), AXES)
    placed = (
        P(None, AXES, None, None, None),
        P(AXES),
        P(AXES, None),
        P(None, AXES),
        P(None, AXES),
        P(AXES),
    )
    return jax.shard_map(local, mesh=split, in_specs=placed, out_specs=(P(AXES), P()), check_vma=False)
```
